32 devices in a mesh: gx: 2 (over y), gy: 4 (over x, core), gz: 4 (over z).
Axes of the slice: x: 2, y: 2, z: 4, core: 2. Of those that a mesh axis runs over, the one named last changes fastest.
Arguments:
- fluid_state: float32 [4, 32, 64, 512], P(None, 'gx', 'gy', 'gz'), may hold values from -6 to 6
- shell_disp: float32 [3, 32768], P(None, ('gy', 'gz')), may hold values from -6 to 6
- quad_weights: float32 [32, 32, 64], P(('gx', 'gy', 'gz')), may hold values from 0.25 to 1
- quad_elements: int32 [32, 32, 64], P(('gx', 'gy', 'gz')), may hold values from 0 to 32767
- owner_cells: int32 [32, 32, 64], P(('gx', 'gy', 'gz')), may hold values from 0 to 32767
- owner_counts: int32 [32, 32], P(('gx', 'gy', 'gz')), may hold values from 0 to 64, as said below
Outputs:
- fluid_out: float32 [4, 32, 64, 512], P(None, 'gx', 'gy', 'gz')
- shell_out: float32 [3, 32768], P(None, ('gy', 'gz'))
The draws below stay inside these ranges and needn't reach their ends.
Inputs may be any that keep to these rules, and one draw needn't show every extreme that they name: `owner_counts`: some owner has 64 live records from every sender; some owner has none from some sender.
All inputs are finite; a program needn't handle non-finite values.
Results may differ from the reference program's by a relative error of at most 0.000023.
Values sent between devices are 32-bit elements; how exact they have to be, the bound alone decides.
A program may use at most 128 MiB of HBM per device.

```python
import math
import jax
import jax.numpy as jnp
from jax import lax

CX = 16
CY = 16
CZ = 128
SLOT = 64
ITERS = 2
RANKS = 32
NSH = 32768
NX = 32
NY = 64
NZ = 512
N_GY = 4
N_GZ = 4


def draw_owner_counts(key, part):
    key_level, key_drop, key_full, key_empty, key_sender = jax.random.split(jax.random.fold_in(key, 7), 5)
    level = jax.random.randint(key_level, (RANKS, 1), SLOT // 2, SLOT + 1)
    drop = jax.random.randint(key_drop, (RANKS, RANKS), 0, SLOT + 1) % (level // 2 + 1)
    counts = level - drop
    full_owner = jax.random.randint(key_full, (), 0, RANKS)
    offset = jax.random.randint(key_empty, (), 1, RANKS)
    empty_owner = (full_owner + offset) % RANKS
    sender = jax.random.randint(key_sender, (), 0, RANKS)
    rows = jnp.arange(RANKS, dtype=jnp.int32)[:, None]
    columns = jnp.arange(RANKS, dtype=jnp.int32)[None, :]
    counts = jnp.where((rows == empty_owner) & (columns == sender), 0, counts)
    return jnp.where(rows == full_owner, SLOT, counts).astype(jnp.int32)


def touch_ends(drawn, own_key, low, high):
    spot = [jax.random.randint(jax.random.fold_in(own_key, axis), (), 0, length) for axis, length in enumerate(drawn.shape)]
    widest = drawn.shape.index(max(drawn.shape))
    beside = spot[:widest] + [(spot[widest] + 1) % drawn.shape[widest]] + spot[widest + 1:]
    return drawn.at[tuple(spot)].set(low).at[tuple(beside)].set(high)


def shard_levels(stream_key, dims, cuts, least, top_value):
    gain = 1.0
    for position, parts in cuts:
        heights = jax.random.uniform(jax.random.fold_in(jax.random.fold_in(stream_key, 6), position), (parts,), jnp.float32, least / len(cuts), top_value / len(cuts))
        gain = gain * jnp.repeat(jnp.exp(heights), dims[position] // parts).reshape((-1,) + (1,) * (len(dims) - 1 - position))
    return gain


def bell_draw(stream_key, dims, scale, limit, cuts=(), kind=jnp.bfloat16):
    loudness = shard_levels(stream_key, dims, cuts, -0.22, 0.18) if cuts else 1.0
    values = jax.random.normal(stream_key, dims, jnp.float32) * scale * loudness
    return jnp.minimum(jnp.maximum(values, -limit), limit).astype(kind)


def setup_inputs(seed: int = 0) -> dict:
    key_of = jax.random.split(jax.random.key(seed), 7)
    return {
        "fluid_state": bell_draw(key_of[0], (4, NX, NY, NZ), 1.0, 6.0, ((1, 2), (2, 4), (3, 4)), jnp.float32),
        "shell_disp": bell_draw(key_of[1], (3, NSH), 1.0, 6.0, ((1, 16),), jnp.float32),
        "quad_weights": jnp.clip(jnp.exp(math.log(1.0) - 1.3862944 * jax.random.uniform(key_of[2], (RANKS, RANKS, SLOT), jnp.float32) ** shard_levels(key_of[2], (RANKS, RANKS, SLOT), ((0, 32),), -0.2, 0.2)), 0.25, 1.0),
        "quad_elements": touch_ends(jax.random.randint(key_of[3], (RANKS, RANKS, SLOT), 0, NSH), jax.random.fold_in(key_of[3], 1), 0, NSH - 1).astype(jnp.int32),
        "owner_cells": touch_ends(jax.random.randint(key_of[4], (RANKS, RANKS, SLOT), 0, CX * CY * CZ), jax.random.fold_in(key_of[4], 1), 0, (CX * CY * CZ) - 1).astype(jnp.int32),
        "owner_counts": draw_owner_counts(jax.random.fold_in(key_of[6], 71), 0),
    }


advection = 0.2
penalty = 0.5
relaxation = 0.05


def smooth_axis(values, axis):
    length = values.shape[axis] - 2
    lower = lax.slice_in_dim(values, 0, length, axis=axis)
    middle = lax.slice_in_dim(values, 1, length + 1, axis=axis)
    upper = lax.slice_in_dim(values, 2, length + 2, axis=axis)
    return 0.25 * lower + 0.5 * middle + 0.25 * upper


def sweep_fluid(padded):
    smoothed = smooth_axis(smooth_axis(smooth_axis(padded, 1), 2), 3)
    center = padded[:, 1:-1, 1:-1, 1:-1]
    grad_x = 0.5 * (padded[:, 2:, 1:-1, 1:-1] - padded[:, :-2, 1:-1, 1:-1])
    grad_y = 0.5 * (padded[:, 1:-1, 2:, 1:-1] - padded[:, 1:-1, :-2, 1:-1])
    grad_z = 0.5 * (padded[:, 1:-1, 1:-1, 2:] - padded[:, 1:-1, 1:-1, :-2])
    convect = center[0:1] * grad_x + center[1:2] * grad_y + center[2:3] * grad_z
    updated = smoothed - advection * convect
    pressure_grad = jnp.stack([grad_x[3], grad_y[3], grad_z[3]])
    return jnp.concatenate([updated[0:3] - advection * pressure_grad, updated[3:4]], 0)


def reference(fluid_state, shell_disp, quad_weights, quad_elements, owner_cells, owner_counts):
    dest_rank = jnp.arange(RANKS, dtype=jnp.int32)[None, :, None]
    cell_ids = jnp.transpose(owner_cells, (1, 0, 2))
    counts_sd = jnp.transpose(owner_counts, (1, 0))
    slot_index = jnp.arange(SLOT, dtype=jnp.int32)[None, None, :]
    live_mask = (slot_index < counts_sd[:, :, None]).astype(jnp.float32)
    brick_x = dest_rank // (N_GY * N_GZ)
    brick_y = (dest_rank // N_GZ) % N_GY
    brick_z = dest_rank % N_GZ
    index_x = brick_x * CX + cell_ids // (CY * CZ)
    index_y = brick_y * CY + (cell_ids // CZ) % CY
    index_z = brick_z * CZ + cell_ids % CZ
    for iteration in range(ITERS):
        padded = jnp.pad(fluid_state, ((0, 0), (1, 1), (1, 1), (1, 1)))
        halfway = sweep_fluid(padded)
        velocity = halfway[0:3, index_x, index_y, index_z]
        shell_vel = shell_disp[:, quad_elements]
        traction = penalty * quad_weights[None] * (velocity - shell_vel) * live_mask[None]
        forcing = jnp.zeros((3, NX, NY, NZ), jnp.float32).at[:, index_x, index_y, index_z].add(traction)
        fluid_state = jnp.concatenate([halfway[0:3] - forcing, halfway[3:4]], 0)
        node_loads = jnp.zeros((3, NSH), jnp.float32).at[:, quad_elements].add(traction)
        shell_disp = shell_disp + relaxation * node_loads
    return fluid_state, shell_disp
```

```python
import functools

import jax
import jax.numpy as jnp
from jax import lax
from jax.experimental import pallas as pl
from jax.experimental.pallas import tpu as pltpu
from jax.sharding import PartitionSpec as P

ITERS = 2

advection = 0.2
penalty = 0.5
relaxation = 0.05
AXES = ("gx", "gy", "gz")
MESH = pl.DeviceIdType.MESH
F32 = jnp.float32
BF16 = jnp.bfloat16


class Place:
    def __init__(self, sizes):
        self.nx, self.ny, self.nz = sizes
        self.plane = self.nx * self.ny
        self.x, self.y, self.z = (lax.axis_index(a) for a in AXES)
        self.p = self.x * self.ny + self.y

    def plane_peer(self, d):
        p = lax.rem(self.p + d, self.plane)
        return p, (lax.div(p, self.ny), lax.rem(p, self.ny), self.z)

    def line_peer(self, d):
        z = lax.rem(self.z + d, self.nz)
        return z, (self.x, self.y, z)

    def barrier(self):
        sem = pltpu.get_barrier_semaphore()
        for d in range(1, self.plane):
            pl.semaphore_signal(sem, inc=1, device_id=self.plane_peer(d)[1], device_id_type=MESH)
        for d in range(1, self.nz):
            pl.semaphore_signal(sem, inc=1, device_id=self.line_peer(d)[1], device_id_type=MESH)
        pl.semaphore_wait(sem, self.plane - 1 + self.nz - 1)


def send(src, dst, sems, k, device):
    return pltpu.make_async_remote_copy(
        src_ref=src, dst_ref=dst, send_sem=sems.at[0, k], recv_sem=sems.at[1, k],
        device_id=device, device_id_type=MESH,
    )


def start_all(copies):
    for c in copies:
        c.start()
    return copies


def wait_all(copies):
    for c in copies:
        c.wait()


class Halo:
    def __init__(self, here, count, device_of, srcs, dsts, sems):
        self.has = (here > 0, here < count - 1)
        self.copies = []
        for s in (0, 1):
            there = jnp.clip(here + (2 * s - 1), 0, count - 1)
            self.copies.append(send(srcs[s], dsts[1 - s], sems, s, device_of(there)))

    def start(self):
        for s in (0, 1):
            @pl.when(self.has[s])
            def _():
                self.copies[s].start()

    def wait(self):
        for s in (0, 1):
            @pl.when(self.has[s])
            def _():
                self.copies[s].wait_send()
                self.copies[1 - s].wait_recv()


class Sweep:
    def __init__(self, at, f, half, fx, sx, sxy, ys, yh, zs, zh, sem_x, sem_y, sem_z):
        self.at, self.f, self.half, self.fx, self.sx, self.sxy = at, f, half, fx, sx, sxy
        self.ys, self.yh, self.zs, self.zh = ys, yh, zs, zh
        self.nf, self.bx, self.by, self.bz = f.shape
        bx = self.bx
        self.hx = Halo(at.x, at.nx, lambda x: (x, at.y, at.z),
                       (f.at[:, 0], f.at[:, bx - 1]), (fx.at[:, 0], fx.at[:, bx + 1]), sem_x)
        self.hy = Halo(at.y, at.ny, lambda y: (at.x, y, at.z),
                       (ys.at[0], ys.at[1]), (yh.at[0], yh.at[1]), sem_y)
        self.hz = Halo(at.z, at.nz, lambda z: (at.x, at.y, z),
                       (zs.at[0], zs.at[1]), (zh.at[0], zh.at[1]), sem_z)

    def start_x(self):
        self.hx.start()
        for s, edge in ((0, 0), (1, self.bx + 1)):
            @pl.when(jnp.logical_not(self.hx.has[s]))
            def _():
                self.fx[:, edge] = jnp.zeros((self.nf, self.by, self.bz), F32)

            @pl.when(jnp.logical_not(self.hy.has[s]))
            def _():
                self.yh[s] = jnp.zeros(self.yh.shape[1:], F32)

            @pl.when(jnp.logical_not(self.hz.has[s]))
            def _():
                self.zh[s] = jnp.zeros(self.zh.shape[1:], F32)
        self.fx[:, 1:self.bx + 1] = self.f[...]

    def x_then_start_y(self):
        self.hx.wait()

        def step(x, _):
            for c in range(self.nf):
                mid = self.fx[c, x + 1]
                s = 0.25 * self.fx[c, x] + 0.5 * mid + 0.25 * self.fx[c, x + 2]
                self.sx[c, x] = s
                row = c * self.bx + x
                self.ys[0, 0, pl.ds(row, 1), :] = mid[0:1]
                self.ys[1, 0, pl.ds(row, 1), :] = mid[self.by - 1:]
                self.ys[0, 1, pl.ds(row, 1), :] = s[0:1]
                self.ys[1, 1, pl.ds(row, 1), :] = s[self.by - 1:]
            return 0

        lax.fori_loop(0, self.bx, step, 0)
        self.hy.start()

    def shift_y(self, tile, c, x, kind):
        sub = lax.broadcasted_iota(jnp.int32, tile.shape, 0)
        row = c * self.bx + x
        lower = jnp.where(sub == 0, self.yh[0, kind, pl.ds(row, 1), :], pltpu.roll(tile, 1, axis=0))
        upper = jnp.where(sub == self.by - 1, self.yh[1, kind, pl.ds(row, 1), :],
                          pltpu.roll(tile, self.by - 1, axis=0))
        return lower, upper

    def y_then_start_z(self):
        self.hy.wait()
        lane = lax.broadcasted_iota(jnp.int32, (self.by, self.zs.shape[2]), 1)
        group = self.nf * self.bx

        def step(x, faces):
            low, high = faces
            for c in range(self.nf):
                tile = self.sx[c, x]
                lower, upper = self.shift_y(tile, c, x, 1)
                s = 0.25 * lower + 0.5 * tile + 0.25 * upper
                self.sxy[c, x] = s
                raw = self.fx[c, x + 1]
                k = c * self.bx + x
                low = jnp.where(lane == k, raw[:, 0:1], low)
                low = jnp.where(lane == k + group, s[:, 0:1], low)
                high = jnp.where(lane == k, raw[:, self.bz - 1:], high)
                high = jnp.where(lane == k + group, s[:, self.bz - 1:], high)
            return low, high

        zero = jnp.zeros(lane.shape, F32)
        low, high = lax.fori_loop(0, self.bx, step, (zero, zero))
        self.zs[0] = low
        self.zs[1] = high
        self.hz.start()

    def finish(self):
        self.hz.wait()
        lane = lax.broadcasted_iota(jnp.int32, (self.by, self.bz), 1)
        width = self.zs.shape[2]
        group = self.nf * self.bx

        def step(x, _):
            turn = lax.rem(width - x, width)
            low, high = (pltpu.roll(self.zh[s], turn, axis=1) for s in (0, 1))

            def shift_z(tile, k):
                lower = jnp.where(lane == 0, low[:, k:k + 1], pltpu.roll(tile, 1, axis=1))
                upper = jnp.where(lane == self.bz - 1, high[:, k:k + 1], pltpu.roll(tile, self.bz - 1, axis=1))
                return lower, upper

            u = [self.fx[c, x + 1] for c in range(3)]
            for c in range(self.nf):
                raw = self.fx[c, x + 1]
                s = self.sxy[c, x]
                lower, upper = shift_z(s, group + c * self.bx)
                smoothed = 0.25 * lower + 0.5 * s + 0.25 * upper
                grad_x = 0.5 * (self.fx[c, x + 2] - self.fx[c, x])
                lower, upper = self.shift_y(raw, c, x, 0)
                grad_y = 0.5 * (upper - lower)
                lower, upper = shift_z(raw, c * self.bx)
                grad_z = 0.5 * (upper - lower)
                self.half[c, x] = smoothed - advection * (u[0] * grad_x + u[1] * grad_y + u[2] * grad_z)
                if c == 3:
                    for v, g in enumerate((grad_x, grad_y, grad_z)):
                        self.half[v, x] = self.half[v, x] - advection * g
            return 0

        lax.fori_loop(0, self.bx, step, 0)


def sweep_scratch(block):
    nf, bx, by, bz = block
    width = -(-2 * nf * bx // 128) * 128
    dma = pltpu.SemaphoreType.DMA((2, 2))
    return [
        pltpu.VMEM((nf, bx + 2, by, bz), F32), pltpu.VMEM(block, F32), pltpu.VMEM(block, F32),
        pltpu.VMEM((2, 2, nf * bx, bz), F32), pltpu.VMEM((2, 2, nf * bx, bz), F32),
        pltpu.VMEM((2, by, width), F32), pltpu.VMEM((2, by, width), F32), dma, dma, dma,
    ]


def gather_line(at, piece, line, sems):
    return start_all([send(piece, line.at[at.z], sems, d - 1, at.line_peer(d)[1]) for d in range(1, at.nz)])


def gather_plane(at, line, nodes, sems):
    return start_all([send(line, nodes.at[at.p], sems, d - 1, at.plane_peer(d)[1]) for d in range(1, at.plane)])


def first_kernel(sizes, f, shell, rec, half, nodes, records, line, rec_line,
                 sem_nl, sem_np, sem_rl, sem_rp, *sweep_refs):
    at = Place(sizes)
    sweep = Sweep(at, f, half, *sweep_refs)
    at.barrier()
    sweep.start_x()
    node_copies = gather_line(at, shell.at[at.x], line, sem_nl)
    rec_copies = []
    for d in range(1, at.nz):
        z, device = at.line_peer(d)
        rec_copies.append(send(rec.at[z], rec_line.at[at.z], sem_rl, d - 1, device))
    start_all(rec_copies)
    line[at.z] = shell[at.x]
    rec_line[at.z] = rec[at.z]
    sweep.x_then_start_y()
    wait_all(node_copies)
    node_copies = gather_plane(at, line, nodes, sem_np)
    wait_all(rec_copies)
    rec_copies = []
    for d in range(1, at.plane):
        p, device = at.plane_peer(d)
        rec_copies.append(send(rec_line.at[:, p], records.at[at.p], sem_rp, d - 1, device))
    start_all(rec_copies)
    nodes[at.p] = line[...]
    records[at.p] = rec_line[:, at.p]
    sweep.y_then_start_z()
    sweep.finish()
    wait_all(node_copies)
    wait_all(rec_copies)


def reduce_plane(at, terms, landed, sems):
    copies = []
    for d in range(1, at.plane):
        p, device = at.plane_peer(d)
        copies.append(send(terms.at[p], landed.at[d - 1], sems, d - 1, device))
    return start_all(copies)


def sum_plane(at, terms, landed, sums):
    total = terms[at.p]
    for d in range(1, at.plane):
        total = total + landed[d - 1]
    sums[...] = total


def reduce_line(at, sums, landed, sems):
    copies = []
    for d in range(1, at.nz):
        z, device = at.line_peer(d)
        copies.append(send(sums.at[z], landed.at[d - 1], sems, d - 1, device))
    return start_all(copies)


def sum_line(at, sums, landed):
    total = sums[at.z]
    for d in range(1, at.nz):
        total = total + landed[d - 1]
    return total


def middle_kernel(sizes, f, shell, terms, half, nodes, mine, landed_p, sums, landed_l, line,
                  sem_rp, sem_rl, sem_nl, sem_np, *sweep_refs):
    at = Place(sizes)
    sweep = Sweep(at, f, half, *sweep_refs)
    at.barrier()
    sweep.start_x()
    copies = reduce_plane(at, terms, landed_p, sem_rp)
    sweep.x_then_start_y()
    wait_all(copies)
    sum_plane(at, terms, landed_p, sums)
    copies = reduce_line(at, sums, landed_l, sem_rl)
    sweep.y_then_start_z()
    wait_all(copies)
    fresh = shell[at.x] + relaxation * sum_line(at, sums, landed_l)
    mine[...] = fresh
    line[at.z] = fresh
    copies = gather_line(at, mine, line, sem_nl)
    sweep.finish()
    wait_all(copies)
    copies = gather_plane(at, line, nodes, sem_np)
    nodes[at.p] = line[...]
    wait_all(copies)


def last_kernel(sizes, shell, terms, out, landed_p, sums, landed_l, mine, sem_rp, sem_rl, sem_g):
    at = Place(sizes)
    at.barrier()
    copies = reduce_plane(at, terms, landed_p, sem_rp)
    wait_all(copies)
    sum_plane(at, terms, landed_p, sums)
    copies = reduce_line(at, sums, landed_l, sem_rl)
    wait_all(copies)
    fresh = shell[...] + relaxation * sum_line(at, sums, landed_l)
    mine[...] = fresh
    copies = []
    for d in range(1, at.nx):
        x = lax.rem(at.x + d, at.nx)
        copies.append(send(mine, out.at[at.x], sem_g, d - 1, (x, at.y, at.z)))
    start_all(copies)
    out[at.x] = fresh
    wait_all(copies)


def couple_kernel(sizes, half, nodes, weights_ids, cells, live, fluid, terms, hs, ns, nf32, acc_f, acc_n):
    nx, ny, nz = sizes
    rp, lp, pr, plane_lanes = piece_split(nx, nodes.shape[3:])
    rows = acc_f.shape[0] // 3
    lanes = acc_f.shape[1]
    size = 3 * rows

    def split_store(ref, c, value):
        hi = value.astype(BF16)
        ref[c * rows:(c + 1) * rows] = hi
        ref[size + c * rows:size + (c + 1) * rows] = (value - hi.astype(F32)).astype(BF16)

    def pieces():
        for g in range(nx):
            r0, l0 = (g // lp) * pr, (g % lp) * plane_lanes
            for y in range(ny):
                for z in range(nz):
                    for c in range(3):
                        r = c * rows + (y * nz + z) * (rp * pr) + r0
                        yield g * ny + y, z, c, slice(r, r + pr), slice(l0, l0 + plane_lanes)

    for p, z, c, r, l in pieces():
        nf32[r, l] = nodes[p, z, c]
    for c in range(3):
        value = half[c]
        bx, by, bz = value.shape
        top = value[:, :by // 2].reshape(bx * by // 2, bz)
        low = value[:, by // 2:].reshape(bx * by // 2, bz)
        split_store(hs, c, jnp.concatenate([top, low], axis=1))
        split_store(ns, c, nf32[c * rows:(c + 1) * rows])
    acc_f[...] = jnp.zeros_like(acc_f)
    acc_n[...] = jnp.zeros_like(acc_n)
    width = cells.shape[1]
    sources = cells.shape[0]
    lane_of = lax.broadcasted_iota(jnp.int32, (lanes, 2 * width), 0)
    row_of = lax.broadcasted_iota(jnp.int32, (rows, 2 * width), 0)
    by, bz = half.shape[2:]
    hy = by // 2
    left = lax.broadcasted_iota(jnp.int32, (1, width), 1) < width // 2

    def chunk(q):
        def both(read):
            return jnp.concatenate([read(2 * q), read(2 * q + 1)], axis=1)

        def weight(i):
            top, bottom = weights_ids[pl.ds(i, 1), :], weights_ids[pl.ds(i + sources, 1), :]
            return jnp.where(left, top, pltpu.roll(bottom, width // 2, axis=1))

        def ident(i):
            top, bottom = weights_ids[pl.ds(i, 1), :], weights_ids[pl.ds(i + sources, 1), :]
            return jnp.where(left, pltpu.roll(top, width // 2, axis=1), bottom)

        factor = penalty * both(weight) * both(lambda i: live[pl.ds(i, 1), :])
        node = both(ident).astype(jnp.int32)
        cell = both(lambda i: cells[pl.ds(i, 1), :])
        z = lax.rem(cell, bz)
        y = lax.rem(lax.div(cell, bz), by)
        x = lax.div(cell, by * bz)
        places = (
            (hs, x * hy + lax.rem(y, hy), lax.div(y, hy) * bz + z),
            (ns, lax.div(node, lanes), lax.rem(node, lanes)),
        )
        hots, masks, values = [], [], []
        for ref, r, l in places:
            hot = jnp.where(lane_of == l, 1.0, 0.0).astype(BF16)
            mask = row_of == r
            found = jnp.dot(ref[...], hot, preferred_element_type=F32)
            found = found[:size] + found[size:]
            values.append([
                jnp.sum(jnp.where(mask, found[c * rows:(c + 1) * rows], 0.0), axis=0, keepdims=True)
                for c in range(3)
            ])
            hots.append(hot)
            masks.append(mask)
        traction = [factor * (values[0][c] - values[1][c]) for c in range(3)]
        high = [t.astype(BF16).astype(F32) for t in traction]
        parts = high + [t - h for t, h in zip(traction, high)]
        for hot, mask, acc in zip(hots, masks, (acc_f, acc_n)):
            spread = jnp.concatenate([jnp.where(mask, t, 0.0).astype(BF16) for t in parts], axis=0)
            out = lax.dot_general(spread, hot, (((1,), (1,)), ((), ())), preferred_element_type=F32)
            acc[...] += out[:size] + out[size:]

    if sources <= 16:
        for q in range(sources // 2):
            chunk(q)
    else:
        pl.loop(0, sources // 2)(chunk)

    for c in range(3):
        force = acc_f[c * rows:(c + 1) * rows]
        bx = half.shape[1]
        fluid[c, :, :hy] = half[c, :, :hy] - force[:, :bz].reshape(bx, hy, bz)
        fluid[c, :, hy:] = half[c, :, hy:] - force[:, bz:].reshape(bx, hy, bz)
    fluid[3] = half[3]
    for p, z, c, r, l in pieces():
        terms[p, z, c] = acc_n[r, l]


def piece_split(nx, tail):
    lp = min(2, nx)
    return nx // lp, lp, tail[0], tail[1]


def on_device(sizes, fluid_state, shell_disp, quad_weights, quad_elements, owner_cells, owner_counts):
    nx, ny, nz = sizes
    plane = nx * ny
    slots = quad_weights.shape[2]
    ranks = quad_weights.shape[1]
    block = fluid_state.shape
    nodes_here = shell_disp.shape[1]
    lanes = 2 * block[3]
    lp = min(2, nx)
    rp = nx // lp
    pr, pw = nodes_here // lanes // rp, lanes // lp
    piece = (3, pr, pw)
    shell = shell_disp.reshape(3, rp, pr, lp, pw).transpose(1, 3, 0, 2, 4).reshape((nx,) + piece)
    rec = jnp.concatenate([quad_weights[0], quad_elements[0].astype(F32)], axis=1)
    rec = rec.reshape(plane, nz, 1, 2 * slots).transpose(1, 0, 2, 3)
    live = (jnp.arange(slots, dtype=jnp.int32)[None, :] < owner_counts[0][:, None]).astype(F32)
    halves = ranks // 2
    live = jnp.concatenate([live[:halves], live[halves:]], axis=1)
    cells = jnp.concatenate([owner_cells[0][:halves], owner_cells[0][halves:]], axis=1)

    vmem = pl.BlockSpec(memory_space=pltpu.VMEM)
    shape = lambda s: jax.ShapeDtypeStruct(s, F32)
    line = (nz,) + piece
    full = (plane,) + line
    sem = lambda n: pltpu.SemaphoreType.DMA((2, max(n, 1)))
    params = lambda i: pltpu.CompilerParams(collective_id=i, has_side_effects=True, vmem_limit_bytes=40 << 20)

    half, nodes, records = pl.pallas_call(
        functools.partial(first_kernel, sizes),
        out_shape=(shape(block), shape(full), shape((plane, nz, 1, 2 * slots))),
        in_specs=[vmem] * 3, out_specs=(vmem,) * 3,
        scratch_shapes=[
            pltpu.VMEM(line, F32), pltpu.VMEM((nz, plane, 1, 2 * slots), F32),
            sem(nz - 1), sem(plane - 1), sem(nz - 1), sem(plane - 1),
        ] + sweep_scratch(block),
        compiler_params=params(0),
    )(fluid_state, shell, rec)
    weights_ids = records.reshape(ranks, 2 * slots)

    rows = ny * nz * rp * pr
    couple = pl.pallas_call(
        functools.partial(couple_kernel, sizes),
        out_shape=(shape(block), shape(full)),
        in_specs=[vmem] * 5, out_specs=(vmem,) * 2,
        scratch_shapes=[
            pltpu.VMEM((6 * rows, lanes), BF16), pltpu.VMEM((6 * rows, lanes), BF16),
            pltpu.VMEM((3 * rows, lanes), F32), pltpu.VMEM((3 * rows, lanes), F32),
            pltpu.VMEM((3 * rows, lanes), F32),
        ],
        compiler_params=pltpu.CompilerParams(vmem_limit_bytes=40 << 20),
    )
    fluid, terms = couple(half, nodes, weights_ids, cells, live)

    reduce_scratch = [pltpu.VMEM((plane - 1,) + line, F32), pltpu.VMEM(line, F32), pltpu.VMEM((nz - 1,) + piece, F32)]
    half, nodes, mine = pl.pallas_call(
        functools.partial(middle_kernel, sizes),
        out_shape=(shape(block), shape(full), shape(piece)),
        in_specs=[vmem] * 3, out_specs=(vmem,) * 3,
        scratch_shapes=reduce_scratch + [
            pltpu.VMEM(line, F32), sem(plane - 1), sem(nz - 1), sem(nz - 1), sem(plane - 1),
        ] + sweep_scratch(block),
        compiler_params=params(1),
    )(fluid, shell, terms)
    fluid, terms = couple(half, nodes, weights_ids, cells, live)

    out = pl.pallas_call(
        functools.partial(last_kernel, sizes),
        out_shape=shape((nx,) + piece),
        in_specs=[vmem] * 2, out_specs=vmem,
        scratch_shapes=reduce_scratch + [pltpu.VMEM(piece, F32), sem(plane - 1), sem(nz - 1), sem(nx - 1)],
        compiler_params=params(2),
    )(mine, terms)
    out = out.reshape(rp, lp, 3, pr, pw).transpose(2, 0, 3, 1, 4).reshape(3, nodes_here)
    return fluid, out


def solution(mesh):
    sizes = tuple(mesh.shape[a] for a in AXES)
    return jax.shard_map(
        functools.partial(on_device, sizes),
        mesh=mesh,
        in_specs=(
            P(None, "gx", "gy", "gz"),
            P(None, ("gy", "gz")),
            P(("gx", "gy", "gz"), None, None),
            P(("gx", "gy", "gz"), None, None),
            P(("gx", "gy", "gz"), None, None),
            P(("gx", "gy", "gz"), None),
        ),
        out_specs=(P(None, "gx", "gy", "gz"), P(None, ("gy", "gz"))),
        check_vma=False,
    )
```

```python
import functools

import jax
import jax.numpy as jnp
from jax import lax
from jax.experimental import pallas as pl
from jax.experimental.pallas import tpu as pltpu
from jax.sharding import PartitionSpec as P

ITERS = 2

advection = 0.2
penalty = 0.5
relaxation = 0.05
AXES = ("gx", "gy", "gz")
MESH = pl.DeviceIdType.MESH
F32 = jnp.float32
BF16 = jnp.bfloat16


class Place:
    def __init__(self, sizes):
        self.nx, self.ny, self.nz = sizes
        self.plane = self.nx * self.ny
        self.x, self.y, self.z = (lax.axis_index(a) for a in AXES)
        self.p = self.x * self.ny + self.y

    def plane_peer(self, d):
        p = lax.rem(self.p + d, self.plane)
        return p, (lax.div(p, self.ny), lax.rem(p, self.ny), self.z)

    def line_peer(self, d):
        z = lax.rem(self.z + d, self.nz)
        return z, (self.x, self.y, z)

    def barrier(self):
        sem = pltpu.get_barrier_semaphore()
        for d in range(1, self.plane):
            pl.semaphore_signal(sem, inc=1, device_id=self.plane_peer(d)[1], device_id_type=MESH)
        for d in range(1, self.nz):
            pl.semaphore_signal(sem, inc=1, device_id=self.line_peer(d)[1], device_id_type=MESH)
        pl.semaphore_wait(sem, self.plane - 1 + self.nz - 1)


def send(src, dst, sems, k, device):
    return pltpu.make_async_remote_copy(
        src_ref=src, dst_ref=dst, send_sem=sems.at[0, k], recv_sem=sems.at[1, k],
        device_id=device, device_id_type=MESH,
    )


def start_all(copies):
    for c in copies:
        c.start()
    return copies


def wait_all(copies):
    for c in copies:
        c.wait()


class Halo:
    def __init__(self, here, count, device_of, srcs, dsts, sems):
        self.has = (here > 0, here < count - 1)
        self.copies = []
        for s in (0, 1):
            there = jnp.clip(here + (2 * s - 1), 0, count - 1)
            self.copies.append(send(srcs[s], dsts[1 - s], sems, s, device_of(there)))

    def start(self):
        for s in (0, 1):
            @pl.when(self.has[s])
            def _():
                self.copies[s].start()

    def wait(self):
        for s in (0, 1):
            @pl.when(self.has[s])
            def _():
                self.copies[s].wait_send()
                self.copies[1 - s].wait_recv()


class Sweep:
    def __init__(self, at, half, fx, sx, sxy, ys, yh, zs, zh, sem_x, sem_y, sem_z):
        self.at, self.half, self.fx, self.sx, self.sxy = at, half, fx, sx, sxy
        self.ys, self.yh, self.zs, self.zh = ys, yh, zs, zh
        self.nf, self.bx, self.by, self.bz = half.shape
        bx = self.bx
        self.hx = Halo(at.x, at.nx, lambda x: (x, at.y, at.z),
                       (fx.at[:, 1], fx.at[:, bx]), (fx.at[:, 0], fx.at[:, bx + 1]), sem_x)
        self.hy = Halo(at.y, at.ny, lambda y: (at.x, y, at.z),
                       (ys.at[0], ys.at[1]), (yh.at[0], yh.at[1]), sem_y)
        self.hz = Halo(at.z, at.nz, lambda z: (at.x, at.y, z),
                       (zs.at[0], zs.at[1]), (zh.at[0], zh.at[1]), sem_z)

    def clear_ends(self):
        for s, edge in ((0, 0), (1, self.bx + 1)):
            @pl.when(jnp.logical_not(self.hx.has[s]))
            def _():
                self.fx[:, edge] = jnp.zeros((self.nf, self.by, self.bz), F32)

            @pl.when(jnp.logical_not(self.hy.has[s]))
            def _():
                self.yh[s] = jnp.zeros(self.yh.shape[1:], F32)

            @pl.when(jnp.logical_not(self.hz.has[s]))
            def _():
                self.zh[s] = jnp.zeros(self.zh.shape[1:], F32)

    def start_x(self):
        self.hx.start()

    def x_then_start_y(self):
        self.hx.wait()

        def step(x, _):
            for c in range(self.nf):
                mid = self.fx[c, x + 1]
                s = 0.25 * self.fx[c, x] + 0.5 * mid + 0.25 * self.fx[c, x + 2]
                self.sx[c, x] = s
                row = c * self.bx + x
                self.ys[0, 0, pl.ds(row, 1), :] = mid[0:1]
                self.ys[1, 0, pl.ds(row, 1), :] = mid[self.by - 1:]
                self.ys[0, 1, pl.ds(row, 1), :] = s[0:1]
                self.ys[1, 1, pl.ds(row, 1), :] = s[self.by - 1:]
            return 0

        lax.fori_loop(0, self.bx, step, 0)
        self.hy.start()

    def shift_y(self, tile, c, x, kind):
        sub = lax.broadcasted_iota(jnp.int32, tile.shape, 0)
        row = c * self.bx + x
        lower = jnp.where(sub == 0, self.yh[0, kind, pl.ds(row, 1), :], pltpu.roll(tile, 1, axis=0))
        upper = jnp.where(sub == self.by - 1, self.yh[1, kind, pl.ds(row, 1), :],
                          pltpu.roll(tile, self.by - 1, axis=0))
        return lower, upper

    def y_then_start_z(self):
        self.hy.wait()
        lane = lax.broadcasted_iota(jnp.int32, (self.by, self.zs.shape[2]), 1)
        group = self.nf * self.bx

        def step(x, faces):
            low, high = faces
            for c in range(self.nf):
                tile = self.sx[c, x]
                lower, upper = self.shift_y(tile, c, x, 1)
                s = 0.25 * lower + 0.5 * tile + 0.25 * upper
                self.sxy[c, x] = s
                raw = self.fx[c, x + 1]
                k = c * self.bx + x
                low = jnp.where(lane == k, raw[:, 0:1], low)
                low = jnp.where(lane == k + group, s[:, 0:1], low)
                high = jnp.where(lane == k, raw[:, self.bz - 1:], high)
                high = jnp.where(lane == k + group, s[:, self.bz - 1:], high)
            return low, high

        zero = jnp.zeros(lane.shape, F32)
        low, high = lax.fori_loop(0, self.bx, step, (zero, zero))
        self.zs[0] = low
        self.zs[1] = high
        self.hz.start()

    def finish(self):
        self.hz.wait()
        lane = lax.broadcasted_iota(jnp.int32, (self.by, self.bz), 1)
        width = self.zs.shape[2]
        group = self.nf * self.bx

        def step(x, _):
            turn = lax.rem(width - x, width)
            low, high = (pltpu.roll(self.zh[s], turn, axis=1) for s in (0, 1))

            def shift_z(tile, k):
                lower = jnp.where(lane == 0, low[:, k:k + 1], pltpu.roll(tile, 1, axis=1))
                upper = jnp.where(lane == self.bz - 1, high[:, k:k + 1], pltpu.roll(tile, self.bz - 1, axis=1))
                return lower, upper

            u = [self.fx[c, x + 1] for c in range(3)]
            for c in range(self.nf):
                raw = self.fx[c, x + 1]
                s = self.sxy[c, x]
                lower, upper = shift_z(s, group + c * self.bx)
                smoothed = 0.25 * lower + 0.5 * s + 0.25 * upper
                grad_x = 0.5 * (self.fx[c, x + 2] - self.fx[c, x])
                lower, upper = self.shift_y(raw, c, x, 0)
                grad_y = 0.5 * (upper - lower)
                lower, upper = shift_z(raw, c * self.bx)
                grad_z = 0.5 * (upper - lower)
                self.half[c, x] = smoothed - advection * (u[0] * grad_x + u[1] * grad_y + u[2] * grad_z)
                if c == 3:
                    for v, g in enumerate((grad_x, grad_y, grad_z)):
                        self.half[v, x] = self.half[v, x] - advection * g
            return 0

        lax.fori_loop(0, self.bx, step, 0)


def sweep_scratch(block):
    nf, bx, by, bz = block
    width = -(-2 * nf * bx // 128) * 128
    dma = pltpu.SemaphoreType.DMA((2, 2))
    return [
        pltpu.VMEM((nf, bx + 2, by, bz), F32), pltpu.VMEM(block, F32), pltpu.VMEM(block, F32),
        pltpu.VMEM((2, 2, nf * bx, bz), F32), pltpu.VMEM((2, 2, nf * bx, bz), F32),
        pltpu.VMEM((2, by, width), F32), pltpu.VMEM((2, by, width), F32), dma, dma, dma,
    ]


def gather_line(at, piece, line, sems):
    return start_all([send(piece, line.at[at.z], sems, d - 1, at.line_peer(d)[1]) for d in range(1, at.nz)])


def gather_plane(at, line, nodes, sems):
    return start_all([send(line, nodes.at[at.p], sems, d - 1, at.plane_peer(d)[1]) for d in range(1, at.plane)])


def reduce_plane(at, terms, landed, sems):
    copies = []
    for d in range(1, at.plane):
        p, device = at.plane_peer(d)
        copies.append(send(terms.at[p], landed.at[d - 1], sems, d - 1, device))
    return start_all(copies)


def sum_plane(at, terms, landed, sums):
    total = terms[at.p]
    for d in range(1, at.plane):
        total = total + landed[d - 1]
    sums[...] = total


def reduce_line(at, sums, landed, sems):
    copies = []
    for d in range(1, at.nz):
        z, device = at.line_peer(d)
        copies.append(send(sums.at[z], landed.at[d - 1], sems, d - 1, device))
    return start_all(copies)


def sum_line(at, sums, landed):
    total = sums[at.z]
    for d in range(1, at.nz):
        total = total + landed[d - 1]
    return total


class Couple:
    def __init__(self, sizes, half, nodes, terms, weights_ids, cells, hs, ns, nf32, acc_f, acc_n, speed):
        self.sizes = sizes
        self.half, self.nodes, self.terms = half, nodes, terms
        self.weights_ids, self.cells = weights_ids, cells
        self.hs, self.ns, self.nf32, self.acc_f, self.acc_n, self.speed = hs, ns, nf32, acc_f, acc_n, speed
        self.rows, self.lanes = acc_f.shape[0] // 3, acc_f.shape[1]
        self.size = 3 * self.rows
        self.sources, self.width = cells.shape
        _, self.bx, self.by, self.bz = half.shape
        self.hy = self.by // 2

    def chunks(self, step):
        if self.sources <= 16:
            for q in range(self.sources // 2):
                step(q)
        else:
            pl.loop(0, self.sources // 2)(step)

    def split_store(self, ref, c, value):
        hi = value.astype(BF16)
        ref[c * self.rows:(c + 1) * self.rows] = hi
        ref[self.size + c * self.rows:self.size + (c + 1) * self.rows] = (value - hi.astype(F32)).astype(BF16)

    def pieces(self):
        nx, ny, nz = self.sizes
        pr, pw = self.nodes.shape[3:]
        lp = min(2, nx)
        rp = nx // lp
        for g in range(nx):
            r0, l0 = (g // lp) * pr, (g % lp) * pw
            for y in range(ny):
                for z in range(nz):
                    for c in range(3):
                        r = c * self.rows + (y * nz + z) * (rp * pr) + r0
                        yield g * ny + y, z, c, slice(r, r + pr), slice(l0, l0 + pw)

    def both(self, read, q):
        return jnp.concatenate([read(2 * q), read(2 * q + 1)], axis=1)

    def cell(self, q):
        return self.both(lambda i: self.cells[pl.ds(i, 1), :], q)

    def pair(self, i):
        return self.weights_ids[i], self.weights_ids[i + self.sources]

    def left(self):
        return lax.broadcasted_iota(jnp.int32, (1, self.width), 1) < self.width // 2

    def weight(self, i):
        top, bottom = self.pair(i)
        return jnp.where(self.left(), top, pltpu.roll(bottom, self.width // 2, axis=1))

    def ident(self, i):
        top, bottom = self.pair(i)
        return jnp.where(self.left(), pltpu.roll(top, self.width // 2, axis=1), bottom)

    def cell_place(self, q):
        cell = self.cell(q)
        y = lax.rem(lax.div(cell, self.bz), self.by)
        x = lax.div(cell, self.by * self.bz)
        return self.hots(x * self.hy + lax.rem(y, self.hy), lax.div(y, self.hy) * self.bz + lax.rem(cell, self.bz))

    def node_place(self, q):
        node = self.both(self.ident, q).astype(jnp.int32)
        return self.hots(lax.div(node, self.lanes), lax.rem(node, self.lanes))

    def hots(self, row, lane):
        lane_of = lax.broadcasted_iota(jnp.int32, (self.lanes, 2 * self.width), 0)
        row_of = lax.broadcasted_iota(jnp.int32, (self.rows, 2 * self.width), 0)
        return jnp.where(lane_of == lane, 1.0, 0.0).astype(BF16), row_of == row

    def find(self, ref, hot, mask):
        found = jnp.dot(ref[...], hot, preferred_element_type=F32)
        found = found[:self.size] + found[self.size:]
        return [
            jnp.sum(jnp.where(mask, found[c * self.rows:(c + 1) * self.rows], 0.0), axis=0, keepdims=True)
            for c in range(3)
        ]

    def spread(self, hot, mask, traction, acc):
        high = [t.astype(BF16).astype(F32) for t in traction]
        parts = high + [t - h for t, h in zip(traction, high)]
        values = jnp.concatenate([jnp.where(mask, t, 0.0).astype(BF16) for t in parts], axis=0)
        out = lax.dot_general(values, hot, (((1,), (1,)), ((), ())), preferred_element_type=F32)
        acc[...] += out[:self.size] + out[self.size:]

    def gather_cells(self):
        for c in range(3):
            value = self.half[c]
            top = value[:, :self.hy].reshape(self.rows, self.bz)
            low = value[:, self.hy:].reshape(self.rows, self.bz)
            self.split_store(self.hs, c, jnp.concatenate([top, low], axis=1))
        self.acc_f[...] = jnp.zeros_like(self.acc_f)
        self.acc_n[...] = jnp.zeros_like(self.acc_n)

        def step(q):
            for c, v in enumerate(self.find(self.hs, *self.cell_place(q))):
                self.speed[q, c:c + 1] = v

        self.chunks(step)

    def nodes_to_terms(self):
        for p, z, c, r, l in self.pieces():
            self.nf32[r, l] = self.nodes[p, z, c]
        for c in range(3):
            self.split_store(self.ns, c, self.nf32[c * self.rows:(c + 1) * self.rows])
        total = self.bx * self.by * self.bz

        def step(q):
            factor = jnp.where(self.cell(q) < total, penalty * self.both(self.weight, q), 0.0)
            hot, mask = self.node_place(q)
            shell = self.find(self.ns, hot, mask)
            traction = [factor * (self.speed[q, c:c + 1] - shell[c]) for c in range(3)]
            for c in range(3):
                self.speed[q, c:c + 1] = traction[c]
            self.spread(hot, mask, traction, self.acc_n)

        self.chunks(step)
        for p, z, c, r, l in self.pieces():
            self.terms[p, z, c] = self.acc_n[r, l]

    def force_cells(self, fluid, first):
        def step(q):
            hot, mask = self.cell_place(q)
            self.spread(hot, mask, [self.speed[q, c:c + 1] for c in range(3)], self.acc_f)

        self.chunks(step)
        bx, hy, bz = self.bx, self.hy, self.bz
        for c in range(3):
            force = self.acc_f[c * self.rows:(c + 1) * self.rows]
            fluid[c, first:first + bx, :hy] = self.half[c, :, :hy] - force[:, :bz].reshape(bx, hy, bz)
            fluid[c, first:first + bx, hy:] = self.half[c, :, hy:] - force[:, bz:].reshape(bx, hy, bz)
        fluid[3, first:first + bx] = self.half[3]


def whole_kernel(sizes, fluid_in, shell_in, rec_in, cells_in, fluid, out, *refs):
    refs = list(refs)
    take = lambda n: [refs.pop(0) for _ in range(n)]
    shell, rec, cells, sem_in = take(4)
    line0, line1, nodes0, nodes1, rec_line, records = take(6)
    halves, terms = take(2), take(2)
    reduce0, reduce1 = take(3), take(3)
    mine, last = take(2)
    sem_nl0, sem_np0, sem_rl, sem_rp = take(4)
    sem_ap0, sem_al0, sem_nl1, sem_np1, sem_ap1, sem_al1, sem_g = take(7)
    couple_refs = take(6)
    sweep_refs = take(10), take(10)
    at = Place(sizes)
    sweeps = [Sweep(at, h, *r) for h, r in zip(halves, sweep_refs)]
    bx = halves[0].shape[1]
    fetches = [
        pltpu.make_async_copy(src, dst, sem_in.at[i])
        for i, (src, dst) in enumerate((
            (fluid_in, sweep_refs[0][0].at[:, 1:bx + 1]), (shell_in, shell), (rec_in, rec), (cells_in, cells)))
    ]
    start_all(fetches)
    for sweep in sweeps:
        sweep.clear_ends()
    at.barrier()
    wait_all(fetches)
    first, second = sweeps
    couples = [Couple(sizes, halves[i], (nodes0, nodes1)[i], terms[i], RecordRows(records), cells, *couple_refs)
               for i in (0, 1)]

    first.start_x()
    node_copies = gather_line(at, shell.at[at.x], line0, sem_nl0)
    rec_copies = []
    for d in range(1, at.nz):
        z, device = at.line_peer(d)
        rec_copies.append(send(rec.at[:, z], rec_line.at[at.z], sem_rl, d - 1, device))
    start_all(rec_copies)
    line0[at.z] = shell[at.x]
    rec_line[at.z] = rec[:, at.z]
    first.x_then_start_y()
    wait_all(node_copies)
    node_copies = gather_plane(at, line0, nodes0, sem_np0)
    wait_all(rec_copies)
    rec_copies = []
    for d in range(1, at.plane):
        p, device = at.plane_peer(d)
        rec_copies.append(send(rec_line.at[:, p], records.at[at.p], sem_rp, d - 1, device))
    start_all(rec_copies)
    nodes0[at.p] = line0[...]
    records[at.p] = rec_line[:, at.p]
    first.y_then_start_z()
    first.finish()
    couples[0].gather_cells()
    wait_all(node_copies)
    wait_all(rec_copies)
    couples[0].nodes_to_terms()

    landed_p, sums, landed_l = reduce0
    copies = reduce_plane(at, terms[0], landed_p, sem_ap0)
    couples[0].force_cells(second.fx, 1)
    second.start_x()
    second.x_then_start_y()
    wait_all(copies)
    sum_plane(at, terms[0], landed_p, sums)
    copies = reduce_line(at, sums, landed_l, sem_al0)
    second.y_then_start_z()
    wait_all(copies)
    fresh = shell[at.x] + relaxation * sum_line(at, sums, landed_l)
    mine[...] = fresh
    line1[at.z] = fresh
    copies = gather_line(at, mine, line1, sem_nl1)
    second.finish()
    wait_all(copies)
    copies = gather_plane(at, line1, nodes1, sem_np1)
    nodes1[at.p] = line1[...]
    couples[1].gather_cells()
    wait_all(copies)
    couples[1].nodes_to_terms()

    landed_p, sums, landed_l = reduce1
    copies = reduce_plane(at, terms[1], landed_p, sem_ap1)
    couples[1].force_cells(fluid, 0)
    wait_all(copies)
    sum_plane(at, terms[1], landed_p, sums)
    copies = reduce_line(at, sums, landed_l, sem_al1)
    wait_all(copies)
    fresh = mine[...] + relaxation * sum_line(at, sums, landed_l)
    last[...] = fresh
    copies = []
    for d in range(1, at.nx):
        x = lax.rem(at.x + d, at.nx)
        copies.append(send(last, out.at[at.x], sem_g, d - 1, (x, at.y, at.z)))
    start_all(copies)
    out[at.x] = fresh
    wait_all(copies)


class RecordRows:
    def __init__(self, records):
        self.records, self.nz = records, records.shape[1]

    def __getitem__(self, i):
        if isinstance(i, int):
            return self.records[i // self.nz, i % self.nz]
        return self.records[lax.div(i, self.nz), lax.rem(i, self.nz)]


def on_device(sizes, fluid_state, shell_disp, quad_weights, quad_elements, owner_cells, owner_counts):
    nx, ny, nz = sizes
    plane = nx * ny
    slots = quad_weights.shape[2]
    ranks = quad_weights.shape[1]
    block = fluid_state.shape
    nodes_here = shell_disp.shape[1]
    lanes = 2 * block[3]
    lp = min(2, nx)
    rp = nx // lp
    pr, pw = nodes_here // lanes // rp, lanes // lp
    piece = (3, pr, pw)
    shell = shell_disp.reshape(3, rp, pr, lp, pw).transpose(1, 3, 0, 2, 4).reshape((nx,) + piece)
    rec = jnp.concatenate([quad_weights[0], quad_elements[0].astype(F32)], axis=1)
    rec = rec.reshape(plane, nz, 1, 2 * slots)
    live = jnp.arange(slots, dtype=jnp.int32)[None, :] < owner_counts[0][:, None]
    cells = jnp.where(live, owner_cells[0], block[1] * block[2] * block[3])
    halves = ranks // 2
    cells = jnp.concatenate([cells[:halves], cells[halves:]], axis=1)

    shape = lambda s: jax.ShapeDtypeStruct(s, F32)
    buf = lambda s: pltpu.VMEM(s, F32)
    line = (nz,) + piece
    full = (plane,) + line
    sem = lambda n: pltpu.SemaphoreType.DMA((2, max(n, 1)))
    reduce_scratch = [buf((plane - 1,) + line), buf(line), buf((nz - 1,) + piece)]
    rows = ny * nz * rp * pr
    scratch = [
        buf(shell.shape), buf(rec.shape), pltpu.VMEM(cells.shape, jnp.int32), pltpu.SemaphoreType.DMA((4,)),
        buf(line), buf(line), buf(full), buf(full), buf((nz, plane, 1, 2 * slots)), buf((plane, nz, 1, 2 * slots)),
        buf(block), buf(block), buf(full), buf(full),
        *reduce_scratch, *reduce_scratch, buf(piece), buf(piece),
        sem(nz - 1), sem(plane - 1), sem(nz - 1), sem(plane - 1),
        sem(plane - 1), sem(nz - 1), sem(nz - 1), sem(plane - 1), sem(plane - 1), sem(nz - 1), sem(nx - 1),
        pltpu.VMEM((6 * rows, lanes), BF16), pltpu.VMEM((6 * rows, lanes), BF16),
        buf((3 * rows, lanes)), buf((3 * rows, lanes)), buf((3 * rows, lanes)), buf((ranks // 4, 3, 4 * slots)),
        *sweep_scratch(block), *sweep_scratch(block),
    ]
    anywhere, vmem = pl.BlockSpec(memory_space=pl.ANY), pl.BlockSpec(memory_space=pltpu.VMEM)
    fluid, out = pl.pallas_call(
        functools.partial(whole_kernel, sizes),
        out_shape=(shape(block), shape((nx,) + piece)),
        in_specs=[anywhere] * 4, out_specs=(vmem, vmem),
        scratch_shapes=scratch,
        compiler_params=pltpu.CompilerParams(collective_id=0, has_side_effects=True, vmem_limit_bytes=56 << 20),
    )(fluid_state, shell, rec, cells)
    out = out.reshape(rp, lp, 3, pr, pw).transpose(2, 0, 3, 1, 4).reshape(3, nodes_here)
    return fluid, out


def solution(mesh):
    sizes = tuple(mesh.shape[a] for a in AXES)
    return jax.shard_map(
        functools.partial(on_device, sizes),
        mesh=mesh,
        in_specs=(
            P(None, "gx", "gy", "gz"),
            P(None, ("gy", "gz")),
            P(("gx", "gy", "gz"), None, None),
            P(("gx", "gy", "gz"), None, None),
            P(("gx", "gy", "gz"), None, None),
            P(("gx", "gy", "gz"), None),
        ),
        out_specs=(P(None, "gx", "gy", "gz"), P(None, ("gy", "gz"))),
        check_vma=False,
    )
```

```python
import functools

import jax
import jax.numpy as jnp
from jax import lax
from jax.experimental import pallas as pl
from jax.experimental.pallas import tpu as pltpu
from jax.sharding import PartitionSpec as P

ITERS = 2

advection = 0.2
penalty = 0.5
relaxation = 0.05
AXES = ("gx", "gy", "gz")
MESH = pl.DeviceIdType.MESH
F32 = jnp.float32
BF16 = jnp.bfloat16


class Place:
    def __init__(self, sizes):
        self.nx, self.ny, self.nz = sizes
        self.plane = self.nx * self.ny
        self.x, self.y, self.z = (lax.axis_index(a) for a in AXES)
        self.p = self.x * self.ny + self.y

    def plane_peer(self, d):
        p = lax.rem(self.p + d, self.plane)
        return p, (lax.div(p, self.ny), lax.rem(p, self.ny), self.z)

    def line_peer(self, d):
        z = lax.rem(self.z + d, self.nz)
        return z, (self.x, self.y, z)

    def greet(self):
        sem = pltpu.get_barrier_semaphore()
        for d in range(1, self.plane):
            pl.semaphore_signal(sem, inc=1, device_id=self.plane_peer(d)[1], device_id_type=MESH)
        for d in range(1, self.nz):
            pl.semaphore_signal(sem, inc=1, device_id=self.line_peer(d)[1], device_id_type=MESH)
        for dx in range(1, self.nx):
            for d in range(1, self.nz):
                pl.semaphore_signal(sem, inc=1, device_id=self.side_peer(dx, d)[1], device_id_type=MESH)

    def meet(self):
        pl.semaphore_wait(pltpu.get_barrier_semaphore(), self.plane - 1 + self.nx * (self.nz - 1))

    def side_peer(self, dx, d):
        x, z = lax.rem(self.x + dx, self.nx), lax.rem(self.z + d, self.nz)
        return z, (x, self.y, z)


def send(src, dst, sems, k, device):
    return pltpu.make_async_remote_copy(
        src_ref=src, dst_ref=dst, send_sem=sems.at[0, k], recv_sem=sems.at[1, k],
        device_id=device, device_id_type=MESH,
    )


def start_all(copies):
    for c in copies:
        c.start()
    return copies


def wait_all(copies):
    for c in copies:
        c.wait()


class Halo:
    def __init__(self, here, count, device_of, srcs, dsts, sems):
        self.has = (here > 0, here < count - 1)
        self.copies = []
        for s in (0, 1):
            there = jnp.clip(here + (2 * s - 1), 0, count - 1)
            self.copies.append(send(srcs[s], dsts[1 - s], sems, s, device_of(there)))

    def start(self):
        for s in (0, 1):
            @pl.when(self.has[s])
            def _():
                self.copies[s].start()

    def wait(self):
        for s in (0, 1):
            @pl.when(self.has[s])
            def _():
                self.copies[s].wait_send()
                self.copies[1 - s].wait_recv()


class Sweep:
    def __init__(self, at, half, fx, sx, sxy, ys, yh, zs, zh, sem_x, sem_y, sem_z):
        self.at, self.half, self.fx, self.sx, self.sxy = at, half, fx, sx, sxy
        self.ys, self.yh, self.zs, self.zh = ys, yh, zs, zh
        self.nf, self.bx, self.by, self.bz = half.shape
        bx = self.bx
        self.hx = Halo(at.x, at.nx, lambda x: (x, at.y, at.z),
                       (fx.at[:, 1], fx.at[:, bx]), (fx.at[:, 0], fx.at[:, bx + 1]), sem_x)
        self.hy = Halo(at.y, at.ny, lambda y: (at.x, y, at.z),
                       (ys.at[0], ys.at[1]), (yh.at[0], yh.at[1]), sem_y)
        self.hz = Halo(at.z, at.nz, lambda z: (at.x, at.y, z),
                       (zs.at[0], zs.at[1]), (zh.at[0], zh.at[1]), sem_z)

    def clear_ends(self):
        for s, edge in ((0, 0), (1, self.bx + 1)):
            @pl.when(jnp.logical_not(self.hx.has[s]))
            def _():
                self.fx[:, edge] = jnp.zeros((self.nf, self.by, self.bz), F32)

            @pl.when(jnp.logical_not(self.hy.has[s]))
            def _():
                self.yh[s] = jnp.zeros(self.yh.shape[1:], F32)

            @pl.when(jnp.logical_not(self.hz.has[s]))
            def _():
                self.zh[s] = jnp.zeros(self.zh.shape[1:], F32)

    def start_x(self):
        self.hx.start()

    def x_then_start_y(self):
        self.hx.wait()

        def step(x, _):
            for c in range(self.nf):
                mid = self.fx[c, x + 1]
                s = 0.25 * self.fx[c, x] + 0.5 * mid + 0.25 * self.fx[c, x + 2]
                self.sx[c, x] = s
                row = c * self.bx + x
                self.ys[0, 0, pl.ds(row, 1), :] = mid[0:1]
                self.ys[1, 0, pl.ds(row, 1), :] = mid[self.by - 1:]
                self.ys[0, 1, pl.ds(row, 1), :] = s[0:1]
                self.ys[1, 1, pl.ds(row, 1), :] = s[self.by - 1:]
            return 0

        lax.fori_loop(0, self.bx, step, 0)
        self.hy.start()

    def shift_y(self, tile, c, x, kind):
        sub = lax.broadcasted_iota(jnp.int32, tile.shape, 0)
        row = c * self.bx + x
        lower = jnp.where(sub == 0, self.yh[0, kind, pl.ds(row, 1), :], pltpu.roll(tile, 1, axis=0))
        upper = jnp.where(sub == self.by - 1, self.yh[1, kind, pl.ds(row, 1), :],
                          pltpu.roll(tile, self.by - 1, axis=0))
        return lower, upper

    def y_then_start_z(self):
        self.hy.wait()
        lane = lax.broadcasted_iota(jnp.int32, (self.by, self.zs.shape[2]), 1)
        group = self.nf * self.bx

        def step(x, faces):
            low, high = faces
            for c in range(self.nf):
                tile = self.sx[c, x]
                lower, upper = self.shift_y(tile, c, x, 1)
                s = 0.25 * lower + 0.5 * tile + 0.25 * upper
                self.sxy[c, x] = s
                raw = self.fx[c, x + 1]
                k = c * self.bx + x
                low = jnp.where(lane == k, raw[:, 0:1], low)
                low = jnp.where(lane == k + group, s[:, 0:1], low)
                high = jnp.where(lane == k, raw[:, self.bz - 1:], high)
                high = jnp.where(lane == k + group, s[:, self.bz - 1:], high)
            return low, high

        zero = jnp.zeros(lane.shape, F32)
        low, high = lax.fori_loop(0, self.bx, step, (zero, zero))
        self.zs[0] = low
        self.zs[1] = high
        self.hz.start()

    def finish(self):
        self.hz.wait()
        lane = lax.broadcasted_iota(jnp.int32, (self.by, self.bz), 1)
        width = self.zs.shape[2]
        group = self.nf * self.bx

        def step(x, _):
            turn = lax.rem(width - x, width)
            low, high = (pltpu.roll(self.zh[s], turn, axis=1) for s in (0, 1))

            def shift_z(tile, k):
                lower = jnp.where(lane == 0, low[:, k:k + 1], pltpu.roll(tile, 1, axis=1))
                upper = jnp.where(lane == self.bz - 1, high[:, k:k + 1], pltpu.roll(tile, self.bz - 1, axis=1))
                return lower, upper

            u = [self.fx[c, x + 1] for c in range(3)]
            for c in range(self.nf):
                raw = self.fx[c, x + 1]
                s = self.sxy[c, x]
                lower, upper = shift_z(s, group + c * self.bx)
                smoothed = 0.25 * lower + 0.5 * s + 0.25 * upper
                grad_x = 0.5 * (self.fx[c, x + 2] - self.fx[c, x])
                lower, upper = self.shift_y(raw, c, x, 0)
                grad_y = 0.5 * (upper - lower)
                lower, upper = shift_z(raw, c * self.bx)
                grad_z = 0.5 * (upper - lower)
                self.half[c, x] = smoothed - advection * (u[0] * grad_x + u[1] * grad_y + u[2] * grad_z)
                if c == 3:
                    for v, g in enumerate((grad_x, grad_y, grad_z)):
                        self.half[v, x] = self.half[v, x] - advection * g
            return 0

        lax.fori_loop(0, self.bx, step, 0)


def sweep_scratch(block):
    nf, bx, by, bz = block
    width = -(-2 * nf * bx // 128) * 128
    dma = pltpu.SemaphoreType.DMA((2, 2))
    return [
        pltpu.VMEM((nf, bx + 2, by, bz), F32), pltpu.VMEM(block, F32), pltpu.VMEM(block, F32),
        pltpu.VMEM((2, 2, nf * bx, bz), F32), pltpu.VMEM((2, 2, nf * bx, bz), F32),
        pltpu.VMEM((2, by, width), F32), pltpu.VMEM((2, by, width), F32), dma, dma, dma,
    ]


class Gather:
    def __init__(self, at, piece, line, nodes, sem_l, sem_p):
        self.at, self.piece, self.line, self.nodes, self.sem_l, self.sem_p = at, piece, line, nodes, sem_l, sem_p
        self.on_plane = []

    def start(self):
        at = self.at
        self.on_line = start_all([
            send(self.piece, self.line.at[at.z], self.sem_l, d - 1, at.line_peer(d)[1]) for d in range(1, at.nz)
        ])
        self.to_plane(0, self.piece, at.z)

    def to_plane(self, k, src, z):
        at = self.at
        self.on_plane += start_all([
            send(src, self.nodes.at[at.p, z], self.sem_p, k * (at.plane - 1) + d - 1, at.plane_peer(d)[1])
            for d in range(1, at.plane)
        ])

    def forward(self):
        at = self.at
        for d in range(1, at.nz):
            self.on_line[d - 1].wait_recv()
            z = lax.rem(at.z + at.nz - d, at.nz)
            self.to_plane(d, self.line.at[z], z)
        self.nodes[at.p, at.z] = self.piece[...]
        for d in range(1, at.nz):
            z = lax.rem(at.z + at.nz - d, at.nz)
            self.nodes[at.p, z] = self.line[z]

    def wait(self):
        for c in self.on_line:
            c.wait_send()
        wait_all(self.on_plane)


class Reduce:
    def __init__(self, at, terms, landed_p, sums, landed_l, sem_p, sem_l):
        self.at, self.terms, self.landed_p, self.sums, self.landed_l = at, terms, landed_p, sums, landed_l
        self.sem_p, self.sem_l = sem_p, sem_l
        self.order = list(range(1, at.nz)) + [0]

    def start(self):
        at = self.at
        self.on_plane = {}
        for k in self.order:
            z = lax.rem(at.z + k, at.nz)
            copies = []
            for d in range(1, at.plane):
                p, device = at.plane_peer(d)
                copies.append(send(self.terms.at[p, z], self.landed_p.at[k, d - 1], self.sem_p,
                                   k * (at.plane - 1) + d - 1, device))
            self.on_plane[k] = start_all(copies)

    def forward(self, spread):
        at = self.at
        self.on_line = []
        for k in self.order:
            z = lax.rem(at.z + k, at.nz)
            total = self.terms[at.p, z]
            for d in range(1, at.plane):
                self.on_plane[k][d - 1].wait_recv()
                total = total + self.landed_p[k, d - 1]
            self.sums[k] = total
            for dx in range(spread):
                if k or dx:
                    self.on_line += start_all([
                        send(self.sums.at[k], self.landed_l.at[dx, k], self.sem_l, dx * at.nz + k,
                             at.side_peer(dx, k)[1])
                    ])

    def wait(self):
        wait_all(self.on_line)
        for copies in self.on_plane.values():
            for c in copies:
                c.wait_send()

    def total(self, dx):
        total = self.sums[0] if dx == 0 else self.landed_l[dx, 0]
        for k in range(1, self.at.nz):
            total = total + self.landed_l[dx, k]
        return total


class Couple:
    def __init__(self, sizes, half, nodes, terms, weights_ids, cells, hs, ns, nf32, acc_f, acc_n, speed):
        self.sizes = sizes
        self.half, self.nodes, self.terms = half, nodes, terms
        self.weights_ids, self.cells = weights_ids, cells
        self.hs, self.ns, self.nf32, self.acc_f, self.acc_n, self.speed = hs, ns, nf32, acc_f, acc_n, speed
        self.rows, self.lanes = acc_f.shape[0] // 3, acc_f.shape[1]
        self.size = 3 * self.rows
        self.sources, self.width = cells.shape
        _, self.bx, self.by, self.bz = half.shape
        self.hy = self.by // 2

    def chunks(self, step):
        if self.sources <= 16:
            for q in range(self.sources // 2):
                step(q)
        else:
            pl.loop(0, self.sources // 2)(step)

    def split_store(self, ref, c, value):
        hi = value.astype(BF16)
        ref[c * self.rows:(c + 1) * self.rows] = hi
        ref[self.size + c * self.rows:self.size + (c + 1) * self.rows] = (value - hi.astype(F32)).astype(BF16)

    def pieces(self):
        nx, ny, nz = self.sizes
        pr, pw = self.nodes.shape[3:]
        lp = min(2, nx)
        rp = nx // lp
        for g in range(nx):
            r0, l0 = (g // lp) * pr, (g % lp) * pw
            for y in range(ny):
                for z in range(nz):
                    for c in range(3):
                        r = c * self.rows + (y * nz + z) * (rp * pr) + r0
                        yield g * ny + y, z, c, slice(r, r + pr), slice(l0, l0 + pw)

    def both(self, read, q):
        return jnp.concatenate([read(2 * q), read(2 * q + 1)], axis=1)

    def cell(self, q):
        return self.both(lambda i: self.cells[pl.ds(i, 1), :], q)

    def pair(self, i):
        return self.weights_ids[i], self.weights_ids[i + self.sources]

    def left(self):
        return lax.broadcasted_iota(jnp.int32, (1, self.width), 1) < self.width // 2

    def weight(self, i):
        top, bottom = self.pair(i)
        return jnp.where(self.left(), top, pltpu.roll(bottom, self.width // 2, axis=1))

    def ident(self, i):
        top, bottom = self.pair(i)
        return jnp.where(self.left(), pltpu.roll(top, self.width // 2, axis=1), bottom)

    def cell_place(self, q):
        cell = self.cell(q)
        y = lax.rem(lax.div(cell, self.bz), self.by)
        x = lax.div(cell, self.by * self.bz)
        return self.hots(x * self.hy + lax.rem(y, self.hy), lax.div(y, self.hy) * self.bz + lax.rem(cell, self.bz))

    def node_place(self, q):
        node = self.both(self.ident, q).astype(jnp.int32)
        return self.hots(lax.div(node, self.lanes), lax.rem(node, self.lanes))

    def hots(self, row, lane):
        lane_of = lax.broadcasted_iota(jnp.int32, (self.lanes, 2 * self.width), 0)
        row_of = lax.broadcasted_iota(jnp.int32, (self.rows, 2 * self.width), 0)
        return jnp.where(lane_of == lane, 1.0, 0.0).astype(BF16), row_of == row

    def find(self, ref, hot, mask):
        found = jnp.dot(ref[...], hot, preferred_element_type=F32)
        found = found[:self.size] + found[self.size:]
        return [
            jnp.sum(jnp.where(mask, found[c * self.rows:(c + 1) * self.rows], 0.0), axis=0, keepdims=True)
            for c in range(3)
        ]

    def spread(self, hot, mask, traction, acc):
        high = [t.astype(BF16).astype(F32) for t in traction]
        parts = high + [t - h for t, h in zip(traction, high)]
        values = jnp.concatenate([jnp.where(mask, t, 0.0).astype(BF16) for t in parts], axis=0)
        out = lax.dot_general(values, hot, (((1,), (1,)), ((), ())), preferred_element_type=F32)
        acc[...] += out[:self.size] + out[self.size:]

    def gather_cells(self):
        for c in range(3):
            value = self.half[c]
            top = value[:, :self.hy].reshape(self.rows, self.bz)
            low = value[:, self.hy:].reshape(self.rows, self.bz)
            self.split_store(self.hs, c, jnp.concatenate([top, low], axis=1))
        self.acc_f[...] = jnp.zeros_like(self.acc_f)
        self.acc_n[...] = jnp.zeros_like(self.acc_n)

        def step(q):
            for c, v in enumerate(self.find(self.hs, *self.cell_place(q))):
                self.speed[q, c:c + 1] = v

        self.chunks(step)

    def nodes_to_terms(self):
        for p, z, c, r, l in self.pieces():
            self.nf32[r, l] = self.nodes[p, z, c]
        for c in range(3):
            self.split_store(self.ns, c, self.nf32[c * self.rows:(c + 1) * self.rows])
        total = self.bx * self.by * self.bz

        def step(q):
            factor = jnp.where(self.cell(q) < total, penalty * self.both(self.weight, q), 0.0)
            hot, mask = self.node_place(q)
            shell = self.find(self.ns, hot, mask)
            traction = [factor * (self.speed[q, c:c + 1] - shell[c]) for c in range(3)]
            for c in range(3):
                self.speed[q, c:c + 1] = traction[c]
            self.spread(hot, mask, traction, self.acc_n)

        self.chunks(step)
        for p, z, c, r, l in self.pieces():
            self.terms[p, z, c] = self.acc_n[r, l]

    def force_cells(self, fluid, first):
        def step(q):
            hot, mask = self.cell_place(q)
            self.spread(hot, mask, [self.speed[q, c:c + 1] for c in range(3)], self.acc_f)

        self.chunks(step)
        bx, hy, bz = self.bx, self.hy, self.bz
        for c in range(3):
            force = self.acc_f[c * self.rows:(c + 1) * self.rows]
            fluid[c, first:first + bx, :hy] = self.half[c, :, :hy] - force[:, :bz].reshape(bx, hy, bz)
            fluid[c, first:first + bx, hy:] = self.half[c, :, hy:] - force[:, bz:].reshape(bx, hy, bz)
        fluid[3, first:first + bx] = self.half[3]


def prepare(sizes, shell_raw, weights, elements, owned, counts, shell, rec, cells, joined, total):
    nx, _, nz = sizes
    pr, pw = shell.shape[2:]
    lp = min(2, nx)
    for g in range(nx):
        for r in range(pr):
            m = ((g // lp) * pr + r) * lp * pw + (g % lp) * pw
            for c in range(3):
                shell[g, c, r:r + 1, :] = shell_raw[c:c + 1, m:m + pw]
    ranks, slots = weights.shape[1:]
    joined[:, :slots] = weights[0]
    joined[:, slots:] = elements[0].astype(F32)
    for i in range(ranks):
        rec[i // nz, i % nz] = joined[i:i + 1, :]
    same = lax.broadcasted_iota(jnp.int32, (ranks, ranks), 0) == lax.broadcasted_iota(jnp.int32, (ranks, ranks), 1)
    count = jnp.sum(jnp.where(same, counts[...].astype(F32), 0.0), axis=1, keepdims=True)
    slot = lax.broadcasted_iota(jnp.int32, (ranks, slots), 1).astype(F32)
    value = jnp.where(slot < count, owned[0], total)
    cells[:, :slots] = value[:ranks // 2]
    cells[:, slots:] = value[ranks // 2:]


def whole_kernel(sizes, fluid_in, shell_in, weights_in, elements_in, owned_in, counts_in, fluid, out, *refs):
    refs = list(refs)
    take = lambda n: [refs.pop(0) for _ in range(n)]
    raw = take(5)
    joined, shell, rec, cells, sem_in = take(5)
    line0, line1, nodes0, nodes1, rec_line, records = take(6)
    halves, terms = take(2), take(2)
    reduce0, reduce1 = take(3), take(3)
    mine, last = take(2)
    sem_nl0, sem_np0, sem_rl, sem_rp = take(4)
    sem_ap0, sem_al0, sem_nl1, sem_np1, sem_ap1, sem_al1 = take(6)
    couple_refs = take(6)
    sweep_refs = take(10), take(10)
    at = Place(sizes)
    at.greet()
    sweeps = [Sweep(at, h, *r) for h, r in zip(halves, sweep_refs)]
    _, bx, by, bz = halves[0].shape
    pairs = [(fluid_in, sweep_refs[0][0].at[:, 1:bx + 1])]
    pairs += list(zip((shell_in, weights_in, elements_in, owned_in, counts_in), raw))
    fetches = start_all([pltpu.make_async_copy(src, dst, sem_in.at[i]) for i, (src, dst) in enumerate(pairs)])
    for sweep in sweeps:
        sweep.clear_ends()
    wait_all(fetches)
    prepare(sizes, *raw, shell, rec, cells, joined, bx * by * bz)
    at.meet()
    first, second = sweeps
    couples = [Couple(sizes, halves[i], (nodes0, nodes1)[i], terms[i], RecordRows(records), cells, *couple_refs)
               for i in (0, 1)]
    nodes = Gather(at, shell.at[at.x], line0, nodes0, sem_nl0, sem_np0)
    first.start_x()
    rec_copies = []
    for d in range(1, at.nz):
        z, device = at.line_peer(d)
        rec_copies.append(send(rec.at[:, z], rec_line.at[at.z], sem_rl, d - 1, device))
    start_all(rec_copies)
    nodes.start()
    rec_line[at.z] = rec[:, at.z]
    first.x_then_start_y()
    wait_all(rec_copies)
    rec_copies = []
    for d in range(1, at.plane):
        p, device = at.plane_peer(d)
        rec_copies.append(send(rec_line.at[:, p], records.at[at.p], sem_rp, d - 1, device))
    start_all(rec_copies)
    nodes.forward()
    records[at.p] = rec_line[:, at.p]
    first.y_then_start_z()
    first.finish()
    couples[0].gather_cells()
    nodes.wait()
    wait_all(rec_copies)
    couples[0].nodes_to_terms()

    loads = Reduce(at, terms[0], *reduce0, sem_ap0, sem_al0)
    loads.start()
    couples[0].force_cells(second.fx, 1)
    second.start_x()
    second.x_then_start_y()
    loads.forward(1)
    second.y_then_start_z()
    loads.wait()
    mine[...] = shell[at.x] + relaxation * loads.total(0)
    nodes = Gather(at, mine, line1, nodes1, sem_nl1, sem_np1)
    nodes.start()
    second.finish()
    nodes.forward()
    couples[1].gather_cells()
    nodes.wait()
    couples[1].nodes_to_terms()

    loads = Reduce(at, terms[1], *reduce1, sem_ap1, sem_al1)
    loads.start()
    couples[1].force_cells(fluid, 0)
    loads.forward(at.nx)
    loads.wait()
    for dx in range(at.nx):
        x = lax.rem(at.x + at.nx - dx, at.nx)
        last[x] = nodes1[x * at.ny + at.y, at.z] + relaxation * loads.total(dx)
    pr, pw = shell.shape[2:]
    lp = min(2, at.nx)
    for g in range(at.nx):
        for r in range(pr):
            m = ((g // lp) * pr + r) * lp * pw + (g % lp) * pw
            for c in range(3):
                out[c:c + 1, m:m + pw] = last[g, c, r:r + 1, :]


class RecordRows:
    def __init__(self, records):
        self.records, self.nz = records, records.shape[1]

    def __getitem__(self, i):
        if isinstance(i, int):
            return self.records[i // self.nz, i % self.nz]
        return self.records[lax.div(i, self.nz), lax.rem(i, self.nz)]


def on_device(sizes, fluid_state, shell_disp, quad_weights, quad_elements, owner_cells, owner_counts):
    nx, ny, nz = sizes
    plane = nx * ny
    slots = quad_weights.shape[2]
    ranks = quad_weights.shape[1]
    block = fluid_state.shape
    nodes_here = shell_disp.shape[1]
    lanes = 2 * block[3]
    lp = min(2, nx)
    rp = nx // lp
    pr, pw = nodes_here // lanes // rp, lanes // lp
    piece = (3, pr, pw)
    rec_shape = (plane, nz, 1, 2 * slots)
    shell_shape = (nx,) + piece
    i32 = lambda s: pltpu.VMEM(s, jnp.int32)

    shape = lambda s: jax.ShapeDtypeStruct(s, F32)
    buf = lambda s: pltpu.VMEM(s, F32)
    line = (nz,) + piece
    full = (plane,) + line
    sem = lambda n: pltpu.SemaphoreType.DMA((2, max(n, 1)))
    reduce_scratch = lambda spread: [buf((nz, plane - 1) + piece), buf(line), buf((spread, nz) + piece)]
    rows = ny * nz * rp * pr
    scratch = [
        buf(shell_disp.shape), buf(quad_weights.shape), i32(quad_elements.shape), i32(owner_cells.shape),
        i32(owner_counts.shape),
        buf((ranks, 2 * slots)), buf(shell_shape), buf(rec_shape), i32((ranks // 2, 2 * slots)),
        pltpu.SemaphoreType.DMA((6,)),
        buf(line), buf(line), buf(full), buf(full), buf((nz, plane, 1, 2 * slots)), buf(rec_shape),
        buf(block), buf(block), buf(full), buf(full),
        *reduce_scratch(1), *reduce_scratch(nx), buf(piece), buf(shell_shape),
        sem(nz - 1), sem(nz * (plane - 1)), sem(nz - 1), sem(plane - 1),
        sem(nz * (plane - 1)), sem(nz), sem(nz - 1), sem(nz * (plane - 1)), sem(nz * (plane - 1)), sem(nx * nz),
        pltpu.VMEM((6 * rows, lanes), BF16), pltpu.VMEM((6 * rows, lanes), BF16),
        buf((3 * rows, lanes)), buf((3 * rows, lanes)), buf((3 * rows, lanes)), buf((ranks // 4, 3, 4 * slots)),
        *sweep_scratch(block), *sweep_scratch(block),
    ]
    anywhere, vmem = pl.BlockSpec(memory_space=pl.ANY), pl.BlockSpec(memory_space=pltpu.VMEM)
    fluid, out = pl.pallas_call(
        functools.partial(whole_kernel, sizes),
        out_shape=(shape(block), shape(shell_disp.shape)),
        in_specs=[anywhere] * 6, out_specs=(vmem, vmem),
        scratch_shapes=scratch,
        compiler_params=pltpu.CompilerParams(collective_id=0, has_side_effects=True, vmem_limit_bytes=56 << 20),
    )(fluid_state, shell_disp, quad_weights, quad_elements, owner_cells, owner_counts)
    return fluid, out


def solution(mesh):
    sizes = tuple(mesh.shape[a] for a in AXES)
    return jax.shard_map(
        functools.partial(on_device, sizes),
        mesh=mesh,
        in_specs=(
            P(None, "gx", "gy", "gz"),
            P(None, ("gy", "gz")),
            P(("gx", "gy", "gz"), None, None),
            P(("gx", "gy", "gz"), None, None),
            P(("gx", "gy", "gz"), None, None),
            P(("gx", "gy", "gz"), None),
        ),
        out_specs=(P(None, "gx", "gy", "gz"), P(None, ("gy", "gz"))),
        check_vma=False,
    )
```

```python
import functools

import jax
import jax.numpy as jnp
from jax import lax
from jax.experimental import pallas as pl
from jax.experimental.pallas import tpu as pltpu
from jax.sharding import PartitionSpec as P

ITERS = 2

advection = 0.2
penalty = 0.5
relaxation = 0.05
AXES = ("gx", "gy", "gz")
MESH = pl.DeviceIdType.MESH
F32 = jnp.float32
BF16 = jnp.bfloat16


class Place:
    def __init__(self, sizes):
        self.nx, self.ny, self.nz = sizes
        self.plane = self.nx * self.ny
        self.x, self.y, self.z = (lax.axis_index(a) for a in AXES)
        self.p = self.x * self.ny + self.y

    def plane_peer(self, d):
        p = lax.rem(self.p + d, self.plane)
        return p, (lax.div(p, self.ny), lax.rem(p, self.ny), self.z)

    def line_peer(self, d):
        z = lax.rem(self.z + d, self.nz)
        return z, (self.x, self.y, z)

    def greet(self):
        sem = pltpu.get_barrier_semaphore()
        for d in range(1, self.plane):
            pl.semaphore_signal(sem, inc=1, device_id=self.plane_peer(d)[1], device_id_type=MESH)
        for d in range(1, self.nz):
            pl.semaphore_signal(sem, inc=1, device_id=self.line_peer(d)[1], device_id_type=MESH)
        for dx in range(1, self.nx):
            for d in range(1, self.nz):
                pl.semaphore_signal(sem, inc=1, device_id=self.side_peer(dx, d)[1], device_id_type=MESH)

    def meet(self):
        pl.semaphore_wait(pltpu.get_barrier_semaphore(), self.plane - 1 + self.nx * (self.nz - 1))

    def side_peer(self, dx, d):
        x, z = lax.rem(self.x + dx, self.nx), lax.rem(self.z + d, self.nz)
        return z, (x, self.y, z)


def send(src, dst, sems, k, device):
    return pltpu.make_async_remote_copy(
        src_ref=src, dst_ref=dst, send_sem=sems.at[0, k], recv_sem=sems.at[1, k],
        device_id=device, device_id_type=MESH,
    )


def start_all(copies):
    for c in copies:
        c.start()
    return copies


def wait_all(copies):
    for c in copies:
        c.wait()


class Halo:
    def __init__(self, here, count, device_of, srcs, dsts, sems):
        self.has = (here > 0, here < count - 1)
        self.copies = []
        for s in (0, 1):
            there = jnp.clip(here + (2 * s - 1), 0, count - 1)
            self.copies.append(send(srcs[s], dsts[1 - s], sems, s, device_of(there)))

    def start(self):
        for s in (0, 1):
            @pl.when(self.has[s])
            def _():
                self.copies[s].start()

    def wait(self):
        for s in (0, 1):
            @pl.when(self.has[s])
            def _():
                self.copies[s].wait_send()
                self.copies[1 - s].wait_recv()


class Sweep:
    def __init__(self, at, half, fx, sx, sxy, ys, yh, zs, zh, sem_x, sem_y, sem_z):
        self.at, self.half, self.fx, self.sx, self.sxy = at, half, fx, sx, sxy
        self.ys, self.yh, self.zs, self.zh = ys, yh, zs, zh
        self.nf, self.bx, self.by, self.bz = half.shape
        bx = self.bx
        self.hx = Halo(at.x, at.nx, lambda x: (x, at.y, at.z),
                       (fx.at[:, 1], fx.at[:, bx]), (fx.at[:, 0], fx.at[:, bx + 1]), sem_x)
        self.hy = Halo(at.y, at.ny, lambda y: (at.x, y, at.z),
                       (ys.at[0], ys.at[1]), (yh.at[0], yh.at[1]), sem_y)
        self.hz = Halo(at.z, at.nz, lambda z: (at.x, at.y, z),
                       (zs.at[0], zs.at[1]), (zh.at[0], zh.at[1]), sem_z)

    def clear_ends(self):
        for s, edge in ((0, 0), (1, self.bx + 1)):
            @pl.when(jnp.logical_not(self.hx.has[s]))
            def _():
                self.fx[:, edge] = jnp.zeros((self.nf, self.by, self.bz), F32)

            @pl.when(jnp.logical_not(self.hy.has[s]))
            def _():
                self.yh[s] = jnp.zeros(self.yh.shape[1:], F32)

            @pl.when(jnp.logical_not(self.hz.has[s]))
            def _():
                self.zh[s] = jnp.zeros(self.zh.shape[1:], F32)

    def start_x(self):
        self.hx.start()

    def x_then_start_y(self):
        self.hx.wait()

        def step(x, _):
            for c in range(self.nf):
                mid = self.fx[c, x + 1]
                s = 0.25 * self.fx[c, x] + 0.5 * mid + 0.25 * self.fx[c, x + 2]
                self.sx[c, x] = s
                row = c * self.bx + x
                self.ys[0, 0, pl.ds(row, 1), :] = mid[0:1]
                self.ys[1, 0, pl.ds(row, 1), :] = mid[self.by - 1:]
                self.ys[0, 1, pl.ds(row, 1), :] = s[0:1]
                self.ys[1, 1, pl.ds(row, 1), :] = s[self.by - 1:]
            return 0

        lax.fori_loop(0, self.bx, step, 0)
        self.hy.start()

    def shift_y(self, tile, c, x, kind):
        sub = lax.broadcasted_iota(jnp.int32, tile.shape, 0)
        row = c * self.bx + x
        lower = jnp.where(sub == 0, self.yh[0, kind, pl.ds(row, 1), :], pltpu.roll(tile, 1, axis=0))
        upper = jnp.where(sub == self.by - 1, self.yh[1, kind, pl.ds(row, 1), :],
                          pltpu.roll(tile, self.by - 1, axis=0))
        return lower, upper

    def y_then_start_z(self):
        self.hy.wait()
        lane = lax.broadcasted_iota(jnp.int32, (self.by, self.zs.shape[2]), 1)
        group = self.nf * self.bx

        def step(x, faces):
            low, high = faces
            for c in range(self.nf):
                tile = self.sx[c, x]
                lower, upper = self.shift_y(tile, c, x, 1)
                s = 0.25 * lower + 0.5 * tile + 0.25 * upper
                self.sxy[c, x] = s
                raw = self.fx[c, x + 1]
                k = c * self.bx + x
                low = jnp.where(lane == k, raw[:, 0:1], low)
                low = jnp.where(lane == k + group, s[:, 0:1], low)
                high = jnp.where(lane == k, raw[:, self.bz - 1:], high)
                high = jnp.where(lane == k + group, s[:, self.bz - 1:], high)
            return low, high

        zero = jnp.zeros(lane.shape, F32)
        low, high = lax.fori_loop(0, self.bx, step, (zero, zero))
        self.zs[0] = low
        self.zs[1] = high
        self.hz.start()

    def finish(self):
        self.hz.wait()
        lane = lax.broadcasted_iota(jnp.int32, (self.by, self.bz), 1)
        width = self.zs.shape[2]
        group = self.nf * self.bx

        def step(x, _):
            turn = lax.rem(width - x, width)
            low, high = (pltpu.roll(self.zh[s], turn, axis=1) for s in (0, 1))

            def shift_z(tile, k):
                lower = jnp.where(lane == 0, low[:, k:k + 1], pltpu.roll(tile, 1, axis=1))
                upper = jnp.where(lane == self.bz - 1, high[:, k:k + 1], pltpu.roll(tile, self.bz - 1, axis=1))
                return lower, upper

            u = [self.fx[c, x + 1] for c in range(3)]
            for c in range(self.nf):
                raw = self.fx[c, x + 1]
                s = self.sxy[c, x]
                lower, upper = shift_z(s, group + c * self.bx)
                smoothed = 0.25 * lower + 0.5 * s + 0.25 * upper
                grad_x = 0.5 * (self.fx[c, x + 2] - self.fx[c, x])
                lower, upper = self.shift_y(raw, c, x, 0)
                grad_y = 0.5 * (upper - lower)
                lower, upper = shift_z(raw, c * self.bx)
                grad_z = 0.5 * (upper - lower)
                self.half[c, x] = smoothed - advection * (u[0] * grad_x + u[1] * grad_y + u[2] * grad_z)
                if c == 3:
                    for v, g in enumerate((grad_x, grad_y, grad_z)):
                        self.half[v, x] = self.half[v, x] - advection * g
            return 0

        lax.fori_loop(0, self.bx, step, 0)


def sweep_scratch(block):
    nf, bx, by, bz = block
    width = -(-2 * nf * bx // 128) * 128
    dma = pltpu.SemaphoreType.DMA((2, 2))
    return [
        pltpu.VMEM((nf, bx + 2, by, bz), F32), pltpu.VMEM(block, F32), pltpu.VMEM(block, F32),
        pltpu.VMEM((2, 2, nf * bx, bz), F32), pltpu.VMEM((2, 2, nf * bx, bz), F32),
        pltpu.VMEM((2, by, width), F32), pltpu.VMEM((2, by, width), F32), dma, dma, dma,
    ]


class Gather:
    def __init__(self, at, piece, line, nodes, sem_l, sem_p):
        self.at, self.piece, self.line, self.nodes, self.sem_l, self.sem_p = at, piece, line, nodes, sem_l, sem_p
        self.on_plane = []

    def start(self):
        at = self.at
        self.on_line = start_all([
            send(self.piece, self.line.at[at.z], self.sem_l, d - 1, at.line_peer(d)[1]) for d in range(1, at.nz)
        ])

    def own(self):
        self.to_plane(0, self.piece, self.at.z)

    def to_plane(self, k, src, z):
        at = self.at
        self.on_plane += start_all([
            send(src, self.nodes.at[at.p, z], self.sem_p, k * (at.plane - 1) + d - 1, at.plane_peer(d)[1])
            for d in range(1, at.plane)
        ])

    def forward(self):
        at = self.at
        for d in range(1, at.nz):
            self.on_line[d - 1].wait_recv()
            z = lax.rem(at.z + at.nz - d, at.nz)
            self.to_plane(d, self.line.at[z], z)
        self.nodes[at.p, at.z] = self.piece[...]
        for d in range(1, at.nz):
            z = lax.rem(at.z + at.nz - d, at.nz)
            self.nodes[at.p, z] = self.line[z]

    def wait(self):
        for c in self.on_line:
            c.wait_send()
        wait_all(self.on_plane)


class Reduce:
    def __init__(self, at, terms, landed_p, sums, landed_l, sem_p, sem_l):
        self.at, self.terms, self.landed_p, self.sums, self.landed_l = at, terms, landed_p, sums, landed_l
        self.sem_p, self.sem_l = sem_p, sem_l
        self.order = list(range(1, at.nz)) + [0]

    def start(self):
        at = self.at
        self.on_plane = {}
        for k in self.order:
            z = lax.rem(at.z + k, at.nz)
            copies = []
            for d in range(1, at.plane):
                p, device = at.plane_peer(d)
                copies.append(send(self.terms.at[p, z], self.landed_p.at[k, d - 1], self.sem_p,
                                   k * (at.plane - 1) + d - 1, device))
            self.on_plane[k] = start_all(copies)

    def forward(self, spread):
        at = self.at
        self.on_line = []
        for k in self.order:
            z = lax.rem(at.z + k, at.nz)
            total = self.terms[at.p, z]
            for d in range(1, at.plane):
                self.on_plane[k][d - 1].wait_recv()
                total = total + self.landed_p[k, d - 1]
            self.sums[k] = total
            for dx in range(spread):
                if k or dx:
                    self.on_line += start_all([
                        send(self.sums.at[k], self.landed_l.at[dx, k], self.sem_l, dx * at.nz + k,
                             at.side_peer(dx, k)[1])
                    ])

    def wait(self):
        wait_all(self.on_line)
        for copies in self.on_plane.values():
            for c in copies:
                c.wait_send()

    def total(self, dx):
        total = self.sums[0] if dx == 0 else self.landed_l[dx, 0]
        for k in range(1, self.at.nz):
            total = total + self.landed_l[dx, k]
        return total


class Couple:
    def __init__(self, sizes, half, nodes, terms, weights_ids, cells, hs, ns, nf32, acc_f, acc_n, speed):
        self.sizes = sizes
        self.half, self.nodes, self.terms = half, nodes, terms
        self.weights_ids, self.cells = weights_ids, cells
        self.hs, self.ns, self.nf32, self.acc_f, self.acc_n, self.speed = hs, ns, nf32, acc_f, acc_n, speed
        self.rows, self.lanes = acc_f.shape[0] // 3, acc_f.shape[1]
        self.size = 3 * self.rows
        self.sources, self.width = cells.shape
        _, self.bx, self.by, self.bz = half.shape
        self.hy = self.by // 2

    def chunks(self, step):
        if self.sources <= 16:
            for q in range(self.sources // 2):
                step(q)
        else:
            pl.loop(0, self.sources // 2)(step)

    def split_store(self, ref, c, value):
        hi = value.astype(BF16)
        ref[c * self.rows:(c + 1) * self.rows] = hi
        ref[self.size + c * self.rows:self.size + (c + 1) * self.rows] = (value - hi.astype(F32)).astype(BF16)

    def pieces(self):
        nx, ny, nz = self.sizes
        pr, pw = self.nodes.shape[3:]
        lp = min(2, nx)
        rp = nx // lp
        for g in range(nx):
            r0, l0 = (g // lp) * pr, (g % lp) * pw
            for y in range(ny):
                for z in range(nz):
                    for c in range(3):
                        r = c * self.rows + (y * nz + z) * (rp * pr) + r0
                        yield g * ny + y, z, c, slice(r, r + pr), slice(l0, l0 + pw)

    def both(self, read, q):
        return jnp.concatenate([read(2 * q), read(2 * q + 1)], axis=1)

    def cell(self, q):
        return self.both(lambda i: self.cells[pl.ds(i, 1), :], q)

    def pair(self, i):
        return self.weights_ids[i], self.weights_ids[i + self.sources]

    def left(self):
        return lax.broadcasted_iota(jnp.int32, (1, self.width), 1) < self.width // 2

    def weight(self, i):
        top, bottom = self.pair(i)
        return jnp.where(self.left(), top, pltpu.roll(bottom, self.width // 2, axis=1))

    def ident(self, i):
        top, bottom = self.pair(i)
        return jnp.where(self.left(), pltpu.roll(top, self.width // 2, axis=1), bottom)

    def cell_place(self, q):
        cell = self.cell(q)
        y = lax.rem(lax.div(cell, self.bz), self.by)
        x = lax.div(cell, self.by * self.bz)
        return self.hots(x * self.hy + lax.rem(y, self.hy), lax.div(y, self.hy) * self.bz + lax.rem(cell, self.bz))

    def node_place(self, q):
        node = self.both(self.ident, q).astype(jnp.int32)
        return self.hots(lax.div(node, self.lanes), lax.rem(node, self.lanes))

    def hots(self, row, lane):
        lane_of = lax.broadcasted_iota(jnp.int32, (self.lanes, 2 * self.width), 0)
        row_of = lax.broadcasted_iota(jnp.int32, (self.rows, 2 * self.width), 0)
        return jnp.where(lane_of == lane, 1.0, 0.0).astype(BF16), row_of == row

    def find(self, ref, hot, mask):
        found = jnp.dot(ref[...], hot, preferred_element_type=F32)
        found = found[:self.size] + found[self.size:]
        return [
            jnp.sum(jnp.where(mask, found[c * self.rows:(c + 1) * self.rows], 0.0), axis=0, keepdims=True)
            for c in range(3)
        ]

    def spread(self, hot, mask, traction, acc):
        high = [t.astype(BF16).astype(F32) for t in traction]
        parts = high + [t - h for t, h in zip(traction, high)]
        values = jnp.concatenate([jnp.where(mask, t, 0.0).astype(BF16) for t in parts], axis=0)
        out = lax.dot_general(values, hot, (((1,), (1,)), ((), ())), preferred_element_type=F32)
        acc[...] += out[:self.size] + out[self.size:]

    def gather_cells(self):
        for c in range(3):
            value = self.half[c]
            top = value[:, :self.hy].reshape(self.rows, self.bz)
            low = value[:, self.hy:].reshape(self.rows, self.bz)
            self.split_store(self.hs, c, jnp.concatenate([top, low], axis=1))
        self.acc_f[...] = jnp.zeros_like(self.acc_f)
        self.acc_n[...] = jnp.zeros_like(self.acc_n)

        def step(q):
            for c, v in enumerate(self.find(self.hs, *self.cell_place(q))):
                self.speed[q, c:c + 1] = v

        self.chunks(step)

    def nodes_to_terms(self):
        for p, z, c, r, l in self.pieces():
            self.nf32[r, l] = self.nodes[p, z, c]
        for c in range(3):
            self.split_store(self.ns, c, self.nf32[c * self.rows:(c + 1) * self.rows])
        total = self.bx * self.by * self.bz

        def step(q):
            factor = jnp.where(self.cell(q) < total, penalty * self.both(self.weight, q), 0.0)
            hot, mask = self.node_place(q)
            shell = self.find(self.ns, hot, mask)
            traction = [factor * (self.speed[q, c:c + 1] - shell[c]) for c in range(3)]
            for c in range(3):
                self.speed[q, c:c + 1] = traction[c]
            self.spread(hot, mask, traction, self.acc_n)

        self.chunks(step)
        for p, z, c, r, l in self.pieces():
            self.terms[p, z, c] = self.acc_n[r, l]

    def force_cells(self, fluid, first):
        def step(q):
            hot, mask = self.cell_place(q)
            self.spread(hot, mask, [self.speed[q, c:c + 1] for c in range(3)], self.acc_f)

        self.chunks(step)
        bx, hy, bz = self.bx, self.hy, self.bz
        for c in range(3):
            force = self.acc_f[c * self.rows:(c + 1) * self.rows]
            fluid[c, first:first + bx, :hy] = self.half[c, :, :hy] - force[:, :bz].reshape(bx, hy, bz)
            fluid[c, first:first + bx, hy:] = self.half[c, :, hy:] - force[:, bz:].reshape(bx, hy, bz)
        fluid[3, first:first + bx] = self.half[3]


def prepare(sizes, shell_raw, weights, elements, owned, counts, shell, rec, cells, joined, total):
    nx, _, nz = sizes
    pr, pw = shell.shape[2:]
    lp = min(2, nx)
    for g in range(nx):
        for r in range(pr):
            m = ((g // lp) * pr + r) * lp * pw + (g % lp) * pw
            for c in range(3):
                shell[g, c, r:r + 1, :] = shell_raw[c:c + 1, m:m + pw]
    ranks, slots = weights.shape[1:]
    joined[:, :slots] = weights[0]
    joined[:, slots:] = elements[0].astype(F32)
    for i in range(ranks):
        rec[i // nz, i % nz] = joined[i:i + 1, :]
    same = lax.broadcasted_iota(jnp.int32, (ranks, ranks), 0) == lax.broadcasted_iota(jnp.int32, (ranks, ranks), 1)
    count = jnp.sum(jnp.where(same, counts[...].astype(F32), 0.0), axis=1, keepdims=True)
    slot = lax.broadcasted_iota(jnp.int32, (ranks, slots), 1).astype(F32)
    value = jnp.where(slot < count, owned[0], total)
    cells[:, :slots] = value[:ranks // 2]
    cells[:, slots:] = value[ranks // 2:]


def whole_kernel(sizes, fluid_in, shell_in, weights_in, elements_in, owned_in, counts_in, fluid, out, *refs):
    refs = list(refs)
    take = lambda n: [refs.pop(0) for _ in range(n)]
    raw = take(5)
    joined, shell, rec, cells, sem_in = take(5)
    line0, line1, nodes0, nodes1, rec_line, records = take(6)
    halves, terms = take(2), take(2)
    reduce0, reduce1 = take(3), take(3)
    mine, last, result = take(3)
    sem_nl0, sem_np0, sem_rl, sem_rp = take(4)
    sem_ap0, sem_al0, sem_nl1, sem_np1, sem_ap1, sem_al1 = take(6)
    couple_refs = take(6)
    sweep_refs = take(10), take(10)
    at = Place(sizes)
    at.greet()
    sweeps = [Sweep(at, h, *r) for h, r in zip(halves, sweep_refs)]
    _, bx, by, bz = halves[0].shape
    pairs = [(fluid_in, sweep_refs[0][0].at[:, 1:bx + 1])]
    pairs += list(zip((shell_in, weights_in, elements_in, owned_in, counts_in), raw))
    fetches = start_all([pltpu.make_async_copy(src, dst, sem_in.at[i]) for i, (src, dst) in enumerate(pairs)])
    for sweep in sweeps:
        sweep.clear_ends()
    wait_all(fetches)
    prepare(sizes, *raw, shell, rec, cells, joined, bx * by * bz)
    at.meet()
    first, second = sweeps
    couples = [Couple(sizes, halves[i], (nodes0, nodes1)[i], terms[i], RecordRows(records), cells, *couple_refs)
               for i in (0, 1)]
    nodes = Gather(at, shell.at[at.x], line0, nodes0, sem_nl0, sem_np0)
    first.start_x()
    rec_copies = []
    for d in range(1, at.nz):
        z, device = at.line_peer(d)
        rec_copies.append(send(rec.at[:, z], rec_line.at[at.z], sem_rl, d - 1, device))
    start_all(rec_copies)
    nodes.start()
    rec_line[at.z] = rec[:, at.z]
    first.x_then_start_y()
    nodes.own()
    wait_all(rec_copies)
    rec_copies = []
    for d in range(1, at.plane):
        p, device = at.plane_peer(d)
        rec_copies.append(send(rec_line.at[:, p], records.at[at.p], sem_rp, d - 1, device))
    start_all(rec_copies)
    nodes.forward()
    records[at.p] = rec_line[:, at.p]
    first.y_then_start_z()
    first.finish()
    couples[0].gather_cells()
    nodes.wait()
    wait_all(rec_copies)
    couples[0].nodes_to_terms()

    loads = Reduce(at, terms[0], *reduce0, sem_ap0, sem_al0)
    loads.start()
    couples[0].force_cells(second.fx, 1)
    second.start_x()
    loads.forward(1)
    second.x_then_start_y()
    loads.wait()
    mine[...] = shell[at.x] + relaxation * loads.total(0)
    nodes = Gather(at, mine, line1, nodes1, sem_nl1, sem_np1)
    nodes.start()
    nodes.own()
    second.y_then_start_z()
    nodes.forward()
    second.finish()
    couples[1].gather_cells()
    nodes.wait()
    couples[1].nodes_to_terms()

    loads = Reduce(at, terms[1], *reduce1, sem_ap1, sem_al1)
    loads.start()
    couples[1].force_cells(result, 0)
    leave = pltpu.make_async_copy(result, fluid, sem_in.at[0])
    leave.start()
    loads.forward(at.nx)
    loads.wait()
    for dx in range(at.nx):
        x = lax.rem(at.x + at.nx - dx, at.nx)
        last[x] = nodes1[x * at.ny + at.y, at.z] + relaxation * loads.total(dx)
    pr, pw = shell.shape[2:]
    lp = min(2, at.nx)
    for g in range(at.nx):
        for r in range(pr):
            m = ((g // lp) * pr + r) * lp * pw + (g % lp) * pw
            for c in range(3):
                out[c:c + 1, m:m + pw] = last[g, c, r:r + 1, :]
    leave.wait()


class RecordRows:
    def __init__(self, records):
        self.records, self.nz = records, records.shape[1]

    def __getitem__(self, i):
        if isinstance(i, int):
            return self.records[i // self.nz, i % self.nz]
        return self.records[lax.div(i, self.nz), lax.rem(i, self.nz)]


def on_device(sizes, fluid_state, shell_disp, quad_weights, quad_elements, owner_cells, owner_counts):
    nx, ny, nz = sizes
    plane = nx * ny
    slots = quad_weights.shape[2]
    ranks = quad_weights.shape[1]
    block = fluid_state.shape
    nodes_here = shell_disp.shape[1]
    lanes = 2 * block[3]
    lp = min(2, nx)
    rp = nx // lp
    pr, pw = nodes_here // lanes // rp, lanes // lp
    piece = (3, pr, pw)
    rec_shape = (plane, nz, 1, 2 * slots)
    shell_shape = (nx,) + piece
    i32 = lambda s: pltpu.VMEM(s, jnp.int32)

    shape = lambda s: jax.ShapeDtypeStruct(s, F32)
    buf = lambda s: pltpu.VMEM(s, F32)
    line = (nz,) + piece
    full = (plane,) + line
    sem = lambda n: pltpu.SemaphoreType.DMA((2, max(n, 1)))
    reduce_scratch = lambda spread: [buf((nz, plane - 1) + piece), buf(line), buf((spread, nz) + piece)]
    rows = ny * nz * rp * pr
    scratch = [
        buf(shell_disp.shape), buf(quad_weights.shape), i32(quad_elements.shape), i32(owner_cells.shape),
        i32(owner_counts.shape),
        buf((ranks, 2 * slots)), buf(shell_shape), buf(rec_shape), i32((ranks // 2, 2 * slots)),
        pltpu.SemaphoreType.DMA((6,)),
        buf(line), buf(line), buf(full), buf(full), buf((nz, plane, 1, 2 * slots)), buf(rec_shape),
        buf(block), buf(block), buf(full), buf(full),
        *reduce_scratch(1), *reduce_scratch(nx), buf(piece), buf(shell_shape), buf(block),
        sem(nz - 1), sem(nz * (plane - 1)), sem(nz - 1), sem(plane - 1),
        sem(nz * (plane - 1)), sem(nz), sem(nz - 1), sem(nz * (plane - 1)), sem(nz * (plane - 1)), sem(nx * nz),
        pltpu.VMEM((6 * rows, lanes), BF16), pltpu.VMEM((6 * rows, lanes), BF16),
        buf((3 * rows, lanes)), buf((3 * rows, lanes)), buf((3 * rows, lanes)), buf((ranks // 4, 3, 4 * slots)),
        *sweep_scratch(block), *sweep_scratch(block),
    ]
    anywhere, vmem = pl.BlockSpec(memory_space=pl.ANY), pl.BlockSpec(memory_space=pltpu.VMEM)
    fluid, out = pl.pallas_call(
        functools.partial(whole_kernel, sizes),
        out_shape=(shape(block), shape(shell_disp.shape)),
        in_specs=[anywhere] * 6, out_specs=(anywhere, vmem),
        scratch_shapes=scratch,
        compiler_params=pltpu.CompilerParams(collective_id=0, has_side_effects=True, vmem_limit_bytes=56 << 20),
    )(fluid_state, shell_disp, quad_weights, quad_elements, owner_cells, owner_counts)
    return fluid, out


def solution(mesh):
    sizes = tuple(mesh.shape[a] for a in AXES)
    return jax.shard_map(
        functools.partial(on_device, sizes),
        mesh=mesh,
        in_specs=(
            P(None, "gx", "gy", "gz"),
            P(None, ("gy", "gz")),
            P(("gx", "gy", "gz"), None, None),
            P(("gx", "gy", "gz"), None, None),
            P(("gx", "gy", "gz"), None, None),
            P(("gx", "gy", "gz"), None),
        ),
        out_specs=(P(None, "gx", "gy", "gz"), P(None, ("gy", "gz"))),
        check_vma=False,
    )
```
